32 devices in a mesh: dp: 2 (over y), expert: 16 (over z, x, core).
Axes of the slice: x: 2, y: 2, z: 4, core: 2. Of those that a mesh axis runs over, the one named last changes fastest.
Arguments:
- grad_out: bfloat16 [4096, 4096], P(('dp', 'expert')), may hold values from -6 to 6
- saved_pre: bfloat16 [4096, 2, 1536], P(('dp', 'expert')), may hold values from -6 to 6
- gate_weight: bfloat16 [4096, 2], P(('dp', 'expert')), may hold values from 0.049804688 to 0.59765625
- routes: int32 [4096, 2], P(('dp', 'expert')), may hold values from 0 to 15, all different within a row; in each aligned block of 128 rows (0 to 127, 128 to 255, ...) at most 20 rows name the same one
- w_down: bfloat16 [16, 768, 4096], P('expert', None, 'dp'), may hold values from -0.09375 to 0.09375
Outputs:
- grad_pre: bfloat16 [4096, 2, 1536], P(('dp', 'expert'))
- grad_gate: bfloat16 [4096, 2], P(('dp', 'expert'))
- grad_down: bfloat16 [16, 768, 4096], P('expert', None, 'dp')
The draws below stay inside these ranges and needn't reach their ends.
Inputs may be any that keep to these rules, and one draw needn't show every extreme that they name: Among the routes of one device's 128 tokens no expert is named more than 20 times, a bound that some block reaches; a token names 2 different experts.
All inputs are finite; a program needn't handle non-finite values.
Results may differ from the reference program's by a relative error of at most 0.0085.
Values may be sent and summed in bfloat16 or wider, within the bound.
A program may use at most 128 MiB of HBM per device.

```python
import math
import jax
import jax.numpy as jnp
import numpy as np
from jax import lax

D = 4096
HID = 768
TOP = 2
TOK_DEV = 128
EXPERTS = 16
CAP = 20
TOKENS = 4096
N_DP = 2
N_EXPERT = 16


def shard_levels(key, dims, split, low, high):
    level, own = 1.0, jax.random.fold_in(key, 6)
    for axis_at, shards_of in split:
        heights = jnp.exp(jax.random.uniform(jax.random.fold_in(own, axis_at), (shards_of,), jnp.float32, low / len(split), high / len(split)))
        level = level * jnp.repeat(heights, dims[axis_at] // shards_of).reshape([-1 if axis == axis_at else 1 for axis in range(len(dims))])
    return level


def shared_out(key, own, number, rows, number_of, top, reach, lean):
    order = jax.random.permutation(key, number_of)
    packed, ordinary = portions_of(number_of, rows * top, reach, lean, True), portions_of(number_of, rows * top, reach, lean, False)
    places = jnp.arange(number_of)

    def named(lengths, rotation):
        used = int((lengths > 0).sum())
        fixed = max(1, used // 4)
        passed = fixed + (places - fixed + rotation * (used - fixed)) % max(1, number_of - fixed)
        return jnp.zeros((number_of,), jnp.int32).at[order[jnp.where(places < fixed, places, passed)]].set(jnp.asarray(lengths, jnp.int32))

    lengths = jnp.where(number % 4 == 0, named(packed, number // 4), named(ordinary, number - number // 4 - 1))
    mixed = jax.random.permutation(jax.random.fold_in(own, 3), number_of)
    giver, taker = mixed[0:number_of // 2 * 2:2], mixed[1:number_of // 2 * 2:2]
    margin = jnp.minimum(lengths[giver] - 1, reach - lengths[taker]) // 2
    margin = jnp.where((giver == order[0]) | (taker == order[0]) | (lengths[taker] == 0), 0, jnp.maximum(margin, 0))
    passed = jax.random.randint(jax.random.fold_in(own, 4), (number_of // 2,), 0, 1 << 20) % (margin + 1)
    lengths = lengths.at[giver].add(-passed).at[taker].add(passed)
    items = jnp.searchsorted(jnp.cumsum(lengths), jnp.arange(rows * top), side="right").astype(jnp.int32)
    grid = items.reshape(top, rows).T
    grid = grid[jax.random.permutation(jax.random.fold_in(own, 1), rows)]
    rotation = jax.random.randint(jax.random.fold_in(own, 2), (rows, 1), 0, top)
    return jnp.take_along_axis(grid, (jnp.arange(top)[None, :] + rotation) % top, axis=1)


def portions_of(number_of, total, most, slope, full):
    loads = [(1 << 20) // math.isqrt(rank ** slope) + 1 for rank in range(1, number_of + 1)]
    largest = most if full else min(most, max(-(-total // number_of), total * loads[0] // sum(loads)))
    least = 1 if total - largest >= number_of - 1 else 0
    holding, rest = [largest] + [least] * (number_of - 1), total - largest - least * (number_of - 1)
    while rest > 0:
        movable = [i for i in range(1, number_of) if holding[i] < largest] or [i for i in range(1, number_of) if holding[i] < most]
        pool, left = sum([loads[i] for i in movable]), rest
        for i in movable:
            extra = min(most - holding[i], max(1, left * loads[i] // pool), rest)
            holding[i] = holding[i] + extra
            rest = rest - extra
    return np.array(holding)


def bell_draw(own_key, extent, spread, most, shards=(), kind=jnp.bfloat16):
    drawn = jax.random.normal(own_key, extent, jnp.float32) * spread
    if len(shards) > 0:
        drawn = shard_levels(own_key, extent, shards, -0.22, 0.18) * drawn
    return jnp.clip(drawn, min=-most, max=most).astype(kind)


def setup_inputs(seed: int = 0) -> dict:
    keys = jax.random.split(jax.random.key(seed), 6)
    grad_out = bell_draw(keys[0], (TOKENS, D), 1.0, 6.0, ((0, 32),))
    saved_pre = bell_draw(keys[1], (TOKENS, TOP, 2 * HID), 1.5, 6.0, ((0, 32),))
    gate_weight = jnp.clip(0.049804688 + 0.54785156 * jax.random.uniform(keys[2], (TOKENS, TOP), jnp.float32) ** shard_levels(keys[2], (TOKENS, TOP), ((0, 32),), -0.2, 0.2), 0.049804688, 0.59765625).astype(jnp.bfloat16)
    routes_keys = jax.random.split(jax.random.fold_in(keys[3], 1), TOKENS // TOK_DEV)
    routes_turns = jax.random.permutation(jax.random.fold_in(keys[3], 3), TOKENS // TOK_DEV)
    routes = jax.vmap(lambda own, number: shared_out(jax.random.fold_in(keys[3], 2), own, number, TOK_DEV, EXPERTS, TOP, CAP, 2))(routes_keys, routes_turns).reshape((TOKENS, TOP))
    w_down = bell_draw(keys[4], (EXPERTS, HID, D), D ** -0.5, 0.09375, ((0, 16), (2, 2)))
    return {"grad_out": grad_out, "saved_pre": saved_pre, "gate_weight": gate_weight, "routes": routes, "w_down": w_down}


def slot_positions(routes_flat, experts, capacity):
    expert_ids = jnp.arange(experts, dtype=jnp.int32)
    onehot = (routes_flat[:, None] == expert_ids[None, :]).astype(jnp.int32)
    rank = jnp.sum((jnp.cumsum(onehot, axis=0) - 1) * onehot, axis=1)
    return (routes_flat * capacity + rank).astype(jnp.int32)


def swiglu_parts(saved, hidden):
    gate_pre = saved[..., :hidden].astype(jnp.float32)
    up_pre = saved[..., hidden:].astype(jnp.float32)
    return gate_pre, up_pre, jax.nn.silu(gate_pre)


def swiglu_grads(saved, weights, contraction, hidden):
    gate_pre, up_pre, active = swiglu_parts(saved, hidden)
    plain = lax.optimization_barrier((active * up_pre).astype(jnp.bfloat16))
    gate_grad = jnp.sum(plain.astype(jnp.float32) * contraction.astype(jnp.float32), axis=-1).astype(jnp.bfloat16)
    back = weights.astype(jnp.float32)[..., None] * contraction.astype(jnp.float32)
    sigma = jax.nn.sigmoid(gate_pre)
    grad_gate_pre = back * up_pre * sigma * (1.0 + gate_pre * (1.0 - sigma))
    grad_up_pre = back * active
    return jnp.concatenate([grad_gate_pre, grad_up_pre], axis=-1).astype(jnp.bfloat16), gate_grad


def scaled_hidden(saved, weights, hidden):
    gate_pre, up_pre, active = swiglu_parts(saved, hidden)
    return (weights.astype(jnp.float32)[..., None] * active * up_pre).astype(jnp.bfloat16)


def reference(grad_out, saved_pre, gate_weight, routes, w_down):
    devices = N_DP * N_EXPERT
    route_count = TOK_DEV * TOP
    per_device = routes.reshape(devices, route_count)
    positions = jax.vmap(lambda row: slot_positions(row, EXPERTS, CAP))(per_device)
    global_ids = jnp.arange(devices * route_count, dtype=jnp.int32).reshape(devices, route_count)
    owners = jnp.zeros((devices, EXPERTS * CAP), jnp.int32)
    owners = owners.at[jnp.arange(devices, dtype=jnp.int32)[:, None], positions].set(global_ids + 1)
    owners = owners.reshape(devices, EXPERTS, CAP).transpose(1, 0, 2).reshape(EXPERTS, devices * CAP)
    saved_flat = saved_pre.reshape(devices * route_count, 2 * HID)
    weight_flat = gate_weight.reshape(devices * route_count)

    def per_expert(item):
        owner_row, weights = item
        filled = owner_row > 0
        route_ids = jnp.maximum(owner_row - 1, 0)
        rows = jnp.where(filled[:, None], jnp.take(grad_out, route_ids // TOP, axis=0), 0)
        saved = jnp.where(filled[:, None], jnp.take(saved_flat, route_ids, axis=0), 0)
        route_weights = jnp.where(filled, jnp.take(weight_flat, route_ids), 0)
        contraction = jnp.dot(rows, weights.T, preferred_element_type=jnp.float32).astype(jnp.bfloat16)
        scaled = scaled_hidden(saved, route_weights, HID)
        gradient = jnp.dot(scaled.T, rows, preferred_element_type=jnp.float32).astype(jnp.bfloat16)
        return contraction, gradient

    contraction_all, grad_down = lax.map(per_expert, (owners, w_down))
    flat_routes = routes.reshape(devices * route_count)
    device_of = jnp.arange(devices * route_count, dtype=jnp.int32) // route_count
    slot_index = (device_of * CAP + (positions.reshape(devices * route_count) - flat_routes * CAP)).astype(jnp.int32)
    contraction = contraction_all[flat_routes, slot_index]
    grad_pre, grad_gate = swiglu_grads(saved_flat, weight_flat, contraction, HID)
    return grad_pre.reshape(TOKENS, TOP, 2 * HID), grad_gate.reshape(TOKENS, TOP), grad_down
```

```python
import functools

import jax
import jax.numpy as jnp
from jax import lax
from jax.experimental import pallas as pl
from jax.experimental.pallas import tpu as pltpu
from jax.sharding import PartitionSpec as P

BF16 = jnp.bfloat16
F32 = jnp.float32


def slot_positions(routes_flat, experts, capacity):
    expert_ids = jnp.arange(experts, dtype=jnp.int32)
    onehot = (routes_flat[:, None] == expert_ids[None, :]).astype(BF16)
    ids = jnp.arange(routes_flat.shape[0], dtype=jnp.int32)
    before = (ids[None, :] < ids[:, None]).astype(BF16)
    counts = dot(before, onehot, ((1,), (0,)))
    rank = jnp.sum(counts * onehot.astype(F32), axis=1).astype(jnp.int32)
    return routes_flat * capacity + rank


def swiglu_parts(saved, hidden):
    gate_pre = saved[..., :hidden].astype(F32)
    up_pre = saved[..., hidden:].astype(F32)
    return (gate_pre, up_pre, jax.nn.silu(gate_pre))


def swiglu_grads(saved, weights, contraction, hidden):
    gate_pre, up_pre, active = swiglu_parts(saved, hidden)
    plain = (active * up_pre).astype(BF16)
    gate_grad = jnp.sum(plain.astype(F32) * contraction.astype(F32), axis=-1).astype(BF16)
    back = weights.astype(F32)[..., None] * contraction.astype(F32)
    sigma = jax.nn.sigmoid(gate_pre)
    grad_gate_pre = back * up_pre * sigma * (1.0 + gate_pre * (1.0 - sigma))
    grad_up_pre = back * active
    return (jnp.concatenate([grad_gate_pre, grad_up_pre], axis=-1).astype(BF16), gate_grad)


def scaled_hidden(saved, weights, hidden):
    gate_pre, up_pre, active = swiglu_parts(saved, hidden)
    return (weights.astype(F32)[..., None] * active * up_pre).astype(BF16)


def dot(a, b, dims):
    return lax.dot_general(a, b, (dims, ((), ())), preferred_element_type=F32)


def on_device_general(grad_out, saved_pre, gate_weight, routes, w_down):
    tokens_dev, top_count = routes.shape
    hidden = w_down.shape[1]
    half = w_down.shape[2]
    experts = lax.axis_size("expert")
    replicas = lax.axis_size("dp")
    capacity = 5 * tokens_dev * top_count // (4 * experts)
    slots = experts * capacity
    positions = slot_positions(routes.reshape(-1), experts, capacity).reshape(tokens_dev, top_count)
    slot_ids = jnp.arange(slots, dtype=jnp.int32)
    picks = [
        (positions[:, k][None, :] == slot_ids[:, None]).astype(BF16) for k in range(top_count)
    ]
    pick = sum(picks[1:], picks[0])
    devices = replicas * experts
    send_rows = jnp.stack(
        [
            dot(pick, grad_out[:, d * half : (d + 1) * half], ((1,), (0,))).astype(BF16)
            for d in range(replicas)
        ]
    ).reshape(devices, capacity, half)
    scaled = scaled_hidden(saved_pre, gate_weight, hidden)
    send_scaled = sum(dot(picks[k], scaled[:, k], ((1,), (0,))) for k in range(top_count))
    send_scaled = send_scaled.astype(BF16).reshape(experts, capacity, hidden)
    rows = lax.all_to_all(send_rows, ("dp", "expert"), split_axis=0, concat_axis=0, tiled=True)
    scaled_in = lax.all_to_all(send_scaled, "expert", split_axis=0, concat_axis=0, tiled=True)
    scaled_in = lax.all_gather(scaled_in.reshape(slots, hidden), "dp", axis=0, tiled=True)
    rows = rows.reshape(devices * capacity, half)
    partial = dot(rows, w_down[0], ((1,), (1,))).astype(BF16).reshape(devices, capacity, hidden)
    parts = lax.all_to_all(partial, ("dp", "expert"), split_axis=0, concat_axis=0, tiled=True)
    parts = parts.reshape(replicas, slots, hidden)
    contraction = jnp.stack(
        [
            sum(dot(picks[k], parts[d], ((0,), (0,))) for d in range(replicas))
            for k in range(top_count)
        ],
        axis=1,
    ).astype(BF16)
    grads, gate_grad = swiglu_grads(saved_pre, gate_weight, contraction, hidden)
    grad_down = dot(scaled_in, rows, ((0,), (0,))).astype(BF16)
    return grads, gate_grad, grad_down[None]


BASE = 16
MESH = pl.DeviceIdType.MESH


def iota(shape, axis):
    return lax.broadcasted_iota(jnp.int32, shape, axis)


def unfold_pick(groups, rest, q):
    shape = (groups * rest, groups * BASE)
    row, col = iota(shape, 0), iota(shape, 1)
    return (col == (row // rest) * BASE + q * rest + row % rest).astype(BF16)


def fold_pick(groups, rest, fold, q):
    shape = (groups * BASE, groups * rest)
    row, col = iota(shape, 0), iota(shape, 1)
    mine = (row // rest) % fold == q
    return (mine & (col == (row // BASE) * rest + row % rest)).astype(BF16)


def slot_keys(experts, rest, far, routes):
    tokens = routes.shape[1]
    names = iota((experts, tokens), 0)
    relative = [(routes[k : k + 1, :] + experts - far) % experts for k in range(2)]
    named = [(relative[k] == names).astype(F32) for k in range(2)]
    before = (iota((tokens, tokens), 0) < iota((tokens, tokens), 1)).astype(BF16)
    counts = dot((named[0] + named[1]).astype(BF16), before, ((1,), (0,)))
    keys = []
    for k in range(2):
        rank = jnp.sum(counts * named[k], axis=0, keepdims=True).astype(jnp.int32)
        keys.append(
            (
                jnp.where(rank < BASE, relative[k] * BASE + rank, -1),
                jnp.where(rank < BASE, -1, relative[k] * rest + rank - BASE),
            )
        )
    return keys


def exchange_kernel(
    experts, rest, fold, s_fold,
    routes, weights, rows_hbm, saved_hbm, w_hbm,
    pre_out, gate_out, down_hbm,
    rows, saved, w, pack, x, z, scaled, s_pack, s, s_rest, s_turn, px_out, px_in, c, r, c_routes,
    grad_gate_factor, grad_up_factor, plain, key_col, left_col, weight_col, gate_col, total, down,
    load_sem, down_sem, ts, rs, tss, rss, tf, rf, tp, rp, tb, rb,
):
    d = lax.axis_index("dp")
    e = lax.axis_index("expert")
    other = 1 - d
    me = d * experts + e
    half_experts = experts // 2
    at = e % half_experts
    near = (e // half_experts) * half_experts
    far = half_experts - near
    tokens, width = rows.shape
    half = width // 2
    part = half // fold
    hidden = w.shape[0]
    part_s = hidden // s_fold
    group = half_experts * BASE
    rest_group = half_experts * rest
    count = experts * BASE

    def block(i):
        return pl.ds(pl.multiple_of(i * BASE, BASE), BASE)

    def remote(src, dst, send, recv, to):
        return pltpu.make_async_remote_copy(
            src_ref=src, dst_ref=dst, send_sem=send, recv_sem=recv, device_id=to, device_id_type=MESH
        )

    def wait_bytes(ref, sem):
        pltpu.make_async_copy(ref, ref, sem).wait()

    def loop(first, last, body):
        def step(k, carry):
            body(k)
            return carry

        lax.fori_loop(first, last, step, 0)

    loads = [
        pltpu.make_async_copy(rows_hbm, rows, load_sem.at[0]),
        pltpu.make_async_copy(saved_hbm, saved, load_sem.at[1]),
        pltpu.make_async_copy(w_hbm, w, load_sem.at[2]),
    ]
    for load in loads:
        load.start()
    barrier = pltpu.get_barrier_semaphore()

    def greet(k):
        p = (me + k) % (2 * experts)
        pl.semaphore_signal(
            barrier, inc=1, device_id=(p // experts, p % experts), device_id_type=MESH
        )

    loop(1, 2 * experts, greet)

    (key0, left0), (key1, left1) = slot_keys(experts, rest, far, routes[...])
    row = iota((count, tokens), 0)
    main_pick = ((key0 == row) | (key1 == row)).astype(BF16)
    slot = (row // BASE) * rest + row % rest
    hit = (left0 == slot) | (left1 == slot)
    left_pick = jnp.concatenate(
        [(hit & ((row // rest) % fold == q)).astype(BF16) for q in range(fold)], axis=1
    )

    def pack_half(side, h):
        def columns(lo, size):
            return pl.ds(pl.multiple_of(h * half + lo, part), size)

        for lo in range(0, half, 512):
            pack[side, :, lo : lo + 512] = dot(
                main_pick, rows[:, columns(lo, 512)], ((1,), (0,))
            ).astype(BF16)
        folded = jnp.concatenate([rows[:, columns(q * part, part)] for q in range(fold)], axis=0)
        pack[side, :, half : half + part] = dot(left_pick, folded, ((1,), (0,))).astype(BF16)

    def row_copy(side, is_far, j):
        g = (0 if is_far else 2) + side
        source = pack.at[side, block(j if is_far else half_experts + j)]
        to = (other if side == 0 else d, (far if is_far else near) + j)
        return remote(source, x.at[block(g * half_experts + at)], ts.at[g], rs.at[g], to)

    loads[0].wait()
    pack_half(0, other)
    pl.semaphore_wait(barrier, 2 * experts - 1)

    def start_across(k):
        j = (at + k) % half_experts
        row_copy(0, True, j).start()
        row_copy(0, False, j).start()

    loop(0, half_experts, start_across)
    pack_half(1, d)

    def start_own(k):
        j = (at + k) % half_experts
        row_copy(1, True, j).start()
        row_copy(1, False, j).start()

    row_copy(1, True, at).start()
    loop(1, half_experts, start_own)
    pltpu.make_async_copy(
        pack.at[1, block(half_experts + at)], x.at[block(3 * half_experts + at)], rs.at[3]
    ).start()

    token_of = iota((2 * tokens, tokens), 0) // 2 == iota((2 * tokens, tokens), 1)
    first = iota((2 * tokens, tokens), 0) % 2 == 0

    def column(v0, v1):
        value = jnp.where(first, v0.astype(F32), v1.astype(F32))
        return jnp.sum(jnp.where(token_of, value, 0.0), axis=1, keepdims=True)

    key_col[...] = column(key0, key1).astype(jnp.int32)
    left_col[...] = column(left0, left1).astype(jnp.int32)
    weight_col[...] = column(weights[0:1, :], weights[1:2, :])
    loads[1].wait()
    step = 16

    @pl.loop(0, tokens // step)
    def _(i):
        mine = pl.ds(pl.multiple_of(i * 2 * step, 2 * step), 2 * step)
        both = saved[pl.ds(pl.multiple_of(i * step, step), step)].reshape(2 * step, 2 * hidden)
        gate_pre = both[:, :hidden].astype(F32)
        up_pre = both[:, hidden:].astype(F32)
        sigma = jax.nn.sigmoid(gate_pre)
        active = gate_pre * sigma
        weight = weight_col[mine, :]
        plain[mine, :] = (active * up_pre).astype(BF16)
        scaled[mine, :] = (weight * active * up_pre).astype(BF16)
        grad_up_factor[mine, :] = weight * active
        grad_gate_factor[mine, :] = weight * up_pre * sigma * (1.0 + gate_pre * (1.0 - sigma))

    slots = iota((2 * tokens, count), 1)

    def route_pick():
        return (key_col[...] == slots).astype(BF16)

    def route_left(q):
        wanted = (slots // BASE) * rest + slots % rest
        mine = (slots // rest) % fold == q
        return (mine & (left_col[...] == wanted)).astype(BF16)

    s_pack[:, 0:hidden] = dot(route_pick(), scaled[...], ((0,), (0,))).astype(BF16)
    folded = jnp.zeros((count, part_s), F32)
    for q in range(s_fold):
        folded = folded + dot(
            route_left(q), scaled[:, q * part_s : (q + 1) * part_s], ((0,), (0,))
        )
    s_pack[:, hidden : hidden + part_s] = folded.astype(BF16)

    def scaled_copy(is_far, j):
        g = 1 if is_far else 3
        n = 0 if is_far else 1
        source = s_pack.at[block(j if is_far else half_experts + j)]
        to = (d, (far if is_far else near) + j)
        return remote(source, s.at[block(g * half_experts + at)], tss.at[n], rss.at[n], to)

    def back_copy(is_far, j):
        n = 0 if is_far else 1
        source = c.at[block(j if is_far else half_experts + j)]
        to = (d, (far if is_far else near) + j)
        return remote(source, r.at[block(n * half_experts + at)], tb.at[n], rb.at[n], to)

    def rows_of(g):
        return slice(g * group, (g + 1) * group)

    def rest_of(g):
        return slice(g * rest_group, (g + 1) * rest_group)

    def contract(g, put):
        wait_bytes(x.at[rows_of(g)], rs.at[g])
        for q in range(fold):
            z[rest_of(g), q * part : (q + 1) * part] = dot(
                unfold_pick(half_experts, rest, q), x[rows_of(g), half : half + part], ((1,), (0,))
            ).astype(BF16)
        lhs = jnp.concatenate([x[rows_of(g), 0:half], z[rest_of(g), :]], axis=0)
        for lo in range(0, hidden, 256):
            put(lo, dot(lhs, w[lo : lo + 256, :], ((1,), (1,))))

    across = (other, e)

    def partial_copy(n):
        return remote(px_out.at[n], px_in.at[n], tp.at[n], rp.at[n], across)

    def forward_copy(n):
        g = 1 + 2 * n
        return remote(s.at[rows_of(g)], s.at[rows_of(g - 1)], tf.at[n], rf.at[n], across)

    loads[2].wait()

    def send_partial(n):
        def put(lo, value):
            px_out[n, :, lo : lo + 256] = value.astype(BF16)

        contract(2 * n, put)
        partial_copy(n).start()

    def finish(n):
        def put(lo, value):
            px_out_cut = slice(lo, lo + 256)
            summed = (value + px_in[n, :, px_out_cut].astype(F32)).astype(BF16)
            c[rows_of(n), px_out_cut] = summed[:group]
            c_routes[0:rest_group, px_out_cut] = summed[group:].astype(F32)

        partial_copy(n).wait_recv()
        contract(2 * n + 1, put)
        folded = jnp.zeros((group, part_s), F32)
        for q in range(s_fold):
            folded = folded + dot(
                fold_pick(half_experts, rest, fold, q),
                c_routes[0:rest_group, q * part_s : (q + 1) * part_s].astype(BF16),
                ((1,), (0,)),
            )
        c[rows_of(n), hidden : hidden + part_s] = folded.astype(BF16)

    send_partial(1)
    send_partial(0)

    def start_scaled(k):
        j = (at + k) % half_experts
        scaled_copy(True, j).start()
        scaled_copy(False, j).start()

    scaled_copy(True, at).start()
    loop(1, half_experts, start_scaled)
    pltpu.make_async_copy(
        s_pack.at[block(half_experts + at)], s.at[block(3 * half_experts + at)], rss.at[1]
    ).start()

    finish(1)

    def start_back_near(k):
        back_copy(False, (at + k) % half_experts).start()

    loop(1, half_experts, start_back_near)
    pltpu.make_async_copy(
        c.at[block(half_experts + at)], r.at[block(half_experts + at)], rb.at[1]
    ).start()
    wait_bytes(s.at[rows_of(3)], rss.at[1])
    forward_copy(1).start()

    finish(0)

    def start_back_far(k):
        back_copy(True, (at + k) % half_experts).start()

    loop(0, half_experts, start_back_far)

    def turn(n):
        for g in (2 * n, 2 * n + 1):
            for q in range(s_fold):
                s_rest[rest_of(g), q * part_s : (q + 1) * part_s] = dot(
                    unfold_pick(half_experts, rest, q),
                    s[rows_of(g), hidden : hidden + part_s],
                    ((1,), (0,)),
                ).astype(BF16)
        s_turn[:, 0 : 2 * group] = s[2 * n * group : (2 * n + 2) * group, 0:hidden].T
        s_turn[:, 2 * group : 2 * group + 2 * rest_group] = s_rest[
            2 * n * rest_group : (2 * n + 2) * rest_group, :
        ].T

    def product(n, columns):
        return dot(
            s_turn[:, 0 : 2 * group], x[2 * n * group : (2 * n + 2) * group, columns], ((1,), (0,))
        ) + dot(
            s_turn[:, 2 * group : 2 * group + 2 * rest_group],
            z[2 * n * rest_group : (2 * n + 2) * rest_group, columns],
            ((1,), (0,)),
        )

    forward_copy(1).wait_recv()
    turn(1)

    @pl.loop(0, half // 512)
    def _(j):
        columns = pl.ds(pl.multiple_of(j * 512, 512), 512)
        total[:, columns] = product(1, columns)

    wait_bytes(s.at[rows_of(1)], rss.at[0])
    forward_copy(0).start()
    forward_copy(0).wait_recv()
    turn(0)

    @pl.loop(0, half // 512)
    def _(j):
        columns = pl.ds(pl.multiple_of(j * 512, 512), 512)
        down[:, columns] = (total[:, columns] + product(0, columns)).astype(BF16)

    store_down = pltpu.make_async_copy(down, down_hbm, down_sem)
    store_down.start()

    wait_bytes(r.at[rows_of(1)], rb.at[1])
    wait_bytes(r.at[rows_of(0)], rb.at[0])
    for q in range(s_fold):
        cut = slice(q * part_s, (q + 1) * part_s)
        c_routes[:, cut] = dot(route_pick(), r[:, cut], ((1,), (0,))) + dot(
            route_left(q), r[:, hidden : hidden + part_s], ((1,), (0,))
        )

    @pl.loop(0, tokens // step)
    def _(i):
        mine = pl.ds(pl.multiple_of(i * 2 * step, 2 * step), 2 * step)
        value = c_routes[mine, :]
        gate_col[mine, :] = jnp.sum(plain[mine, :].astype(F32) * value, axis=1, keepdims=True)
        out = jnp.concatenate(
            [value * grad_gate_factor[mine, :], value * grad_up_factor[mine, :]], axis=1
        ).astype(BF16)
        pre_out[pl.ds(pl.multiple_of(i * step, step), step)] = out.reshape(step, 2, 2 * hidden)

    for k in range(2):
        mine = token_of & (first if k == 0 else ~first)
        gate_out[k : k + 1, :] = jnp.sum(
            jnp.where(mine, gate_col[...], 0.0), axis=0, keepdims=True
        ).astype(BF16)

    wait_bytes(pack.at[0, 0:group], ts.at[0])
    wait_bytes(pack.at[1, 0:group], ts.at[1])
    wait_bytes(pack.at[0, group : 2 * group], ts.at[2])
    wait_bytes(pack.at[1, group : 2 * group - BASE], ts.at[3])
    wait_bytes(s_pack.at[0:group], tss.at[0])
    wait_bytes(s_pack.at[group : 2 * group - BASE], tss.at[1])
    wait_bytes(c.at[0:group], tb.at[0])
    wait_bytes(c.at[group : 2 * group - BASE], tb.at[1])
    for n in range(2):
        partial_copy(n).wait_send()
        forward_copy(n).wait_send()
    store_down.wait()


def on_device(grad_out, saved_pre, gate_weight, routes, w_down):
    tokens, top_count = routes.shape
    hidden, half = w_down.shape[1:]
    width = grad_out.shape[1]
    experts = lax.axis_size("expert")
    replicas = lax.axis_size("dp")
    capacity = 5 * tokens * top_count // (4 * experts)
    if (replicas, top_count, experts, capacity, hidden, half % 512) != (2, 2, 16, 20, 768, 0):
        return on_device_general(grad_out, saved_pre, gate_weight, routes, w_down)
    rest = capacity - BASE
    fold = BASE // rest
    s_fold = hidden // 256
    devices = replicas * experts
    count, total = experts * BASE, devices * BASE
    part, part_s = half // fold, hidden // s_fold
    finished = (count + experts * rest) // 2
    vmem = pl.BlockSpec(memory_space=pltpu.VMEM)
    anywhere = pl.BlockSpec(memory_space=pl.ANY)
    dma = pltpu.SemaphoreType.DMA
    pre, gate, down = pl.pallas_call(
        functools.partial(exchange_kernel, experts, rest, fold, s_fold),
        out_shape=(
            jax.ShapeDtypeStruct(saved_pre.shape, BF16),
            jax.ShapeDtypeStruct((top_count, tokens), BF16),
            jax.ShapeDtypeStruct((hidden, half), BF16),
        ),
        in_specs=[vmem, vmem, anywhere, anywhere, anywhere],
        out_specs=[vmem, vmem, anywhere],
        scratch_shapes=[
            pltpu.VMEM((tokens, width), BF16),
            pltpu.VMEM(saved_pre.shape, BF16),
            pltpu.VMEM((hidden, half), BF16),
            pltpu.VMEM((2, count, half + part), BF16),
            pltpu.VMEM((total, half + part), BF16),
            pltpu.VMEM((devices * rest, half), BF16),
            pltpu.VMEM((2 * tokens, hidden), BF16),
            pltpu.VMEM((count, hidden + part_s), BF16),
            pltpu.VMEM((total, hidden + part_s), BF16),
            pltpu.VMEM((devices * rest, hidden), BF16),
            pltpu.VMEM((hidden, finished * 2), BF16),
            pltpu.VMEM((2, finished, hidden), BF16),
            pltpu.VMEM((2, finished, hidden), BF16),
            pltpu.VMEM((count, hidden + part_s), BF16),
            pltpu.VMEM((count, hidden + part_s), BF16),
            pltpu.VMEM((2 * tokens, hidden), F32),
            pltpu.VMEM((2 * tokens, hidden), F32),
            pltpu.VMEM((2 * tokens, hidden), F32),
            pltpu.VMEM((2 * tokens, hidden), BF16),
            pltpu.VMEM((2 * tokens, 1), jnp.int32),
            pltpu.VMEM((2 * tokens, 1), jnp.int32),
            pltpu.VMEM((2 * tokens, 1), F32),
            pltpu.VMEM((2 * tokens, 1), F32),
            pltpu.VMEM((hidden, half), F32),
            pltpu.VMEM((hidden, half), BF16),
            dma((3,)), dma,
            dma((4,)), dma((4,)),
            dma((2,)), dma((2,)), dma((2,)), dma((2,)),
            dma((2,)), dma((2,)), dma((2,)), dma((2,)),
        ],
        compiler_params=pltpu.CompilerParams(
            collective_id=0, has_side_effects=True, vmem_limit_bytes=48 << 20
        ),
    )(routes.T, gate_weight.T, grad_out, saved_pre, w_down[0])
    return pre, gate.T, down[None]


def solution(mesh):
    return jax.shard_map(
        on_device,
        mesh=mesh,
        in_specs=(
            P(("dp", "expert"), None),
            P(("dp", "expert"), None, None),
            P(("dp", "expert"), None),
            P(("dp", "expert"), None),
            P("expert", None, "dp"),
        ),
        out_specs=(
            P(("dp", "expert"), None, None),
            P(("dp", "expert"), None),
            P("expert", None, "dp"),
        ),
        check_vma=False,
    )
```

```python
import functools

import jax
import jax.numpy as jnp
from jax import lax
from jax.experimental import pallas as pl
from jax.experimental.pallas import tpu as pltpu
from jax.sharding import PartitionSpec as P

BF16 = jnp.bfloat16
F32 = jnp.float32


def slot_positions(routes_flat, experts, capacity):
    expert_ids = jnp.arange(experts, dtype=jnp.int32)
    onehot = (routes_flat[:, None] == expert_ids[None, :]).astype(BF16)
    ids = jnp.arange(routes_flat.shape[0], dtype=jnp.int32)
    before = (ids[None, :] < ids[:, None]).astype(BF16)
    counts = dot(before, onehot, ((1,), (0,)))
    rank = jnp.sum(counts * onehot.astype(F32), axis=1).astype(jnp.int32)
    return routes_flat * capacity + rank


def swiglu_parts(saved, hidden):
    gate_pre = saved[..., :hidden].astype(F32)
    up_pre = saved[..., hidden:].astype(F32)
    return (gate_pre, up_pre, jax.nn.silu(gate_pre))


def swiglu_grads(saved, weights, contraction, hidden):
    gate_pre, up_pre, active = swiglu_parts(saved, hidden)
    plain = (active * up_pre).astype(BF16)
    gate_grad = jnp.sum(plain.astype(F32) * contraction.astype(F32), axis=-1).astype(BF16)
    back = weights.astype(F32)[..., None] * contraction.astype(F32)
    sigma = jax.nn.sigmoid(gate_pre)
    grad_gate_pre = back * up_pre * sigma * (1.0 + gate_pre * (1.0 - sigma))
    grad_up_pre = back * active
    return (jnp.concatenate([grad_gate_pre, grad_up_pre], axis=-1).astype(BF16), gate_grad)


def scaled_hidden(saved, weights, hidden):
    gate_pre, up_pre, active = swiglu_parts(saved, hidden)
    return (weights.astype(F32)[..., None] * active * up_pre).astype(BF16)


def dot(a, b, dims):
    return lax.dot_general(a, b, (dims, ((), ())), preferred_element_type=F32)


def on_device_general(grad_out, saved_pre, gate_weight, routes, w_down):
    tokens_dev, top_count = routes.shape
    hidden = w_down.shape[1]
    half = w_down.shape[2]
    experts = lax.axis_size("expert")
    replicas = lax.axis_size("dp")
    capacity = 5 * tokens_dev * top_count // (4 * experts)
    slots = experts * capacity
    positions = slot_positions(routes.reshape(-1), experts, capacity).reshape(tokens_dev, top_count)
    slot_ids = jnp.arange(slots, dtype=jnp.int32)
    picks = [
        (positions[:, k][None, :] == slot_ids[:, None]).astype(BF16) for k in range(top_count)
    ]
    pick = sum(picks[1:], picks[0])
    devices = replicas * experts
    send_rows = jnp.stack(
        [
            dot(pick, grad_out[:, d * half : (d + 1) * half], ((1,), (0,))).astype(BF16)
            for d in range(replicas)
        ]
    ).reshape(devices, capacity, half)
    scaled = scaled_hidden(saved_pre, gate_weight, hidden)
    send_scaled = sum(dot(picks[k], scaled[:, k], ((1,), (0,))) for k in range(top_count))
    send_scaled = send_scaled.astype(BF16).reshape(experts, capacity, hidden)
    rows = lax.all_to_all(send_rows, ("dp", "expert"), split_axis=0, concat_axis=0, tiled=True)
    scaled_in = lax.all_to_all(send_scaled, "expert", split_axis=0, concat_axis=0, tiled=True)
    scaled_in = lax.all_gather(scaled_in.reshape(slots, hidden), "dp", axis=0, tiled=True)
    rows = rows.reshape(devices * capacity, half)
    partial = dot(rows, w_down[0], ((1,), (1,))).astype(BF16).reshape(devices, capacity, hidden)
    parts = lax.all_to_all(partial, ("dp", "expert"), split_axis=0, concat_axis=0, tiled=True)
    parts = parts.reshape(replicas, slots, hidden)
    contraction = jnp.stack(
        [
            sum(dot(picks[k], parts[d], ((0,), (0,))) for d in range(replicas))
            for k in range(top_count)
        ],
        axis=1,
    ).astype(BF16)
    grads, gate_grad = swiglu_grads(saved_pre, gate_weight, contraction, hidden)
    grad_down = dot(scaled_in, rows, ((0,), (0,))).astype(BF16)
    return grads, gate_grad, grad_down[None]


BASE = 16
MESH = pl.DeviceIdType.MESH


def iota(shape, axis):
    return lax.broadcasted_iota(jnp.int32, shape, axis)


def unfold_pick(groups, rest, q):
    shape = (groups * rest, groups * BASE)
    row, col = iota(shape, 0), iota(shape, 1)
    return (col == (row // rest) * BASE + q * rest + row % rest).astype(BF16)


def fold_pick(groups, rest, fold, q):
    shape = (groups * BASE, groups * rest)
    row, col = iota(shape, 0), iota(shape, 1)
    mine = (row // rest) % fold == q
    return (mine & (col == (row // BASE) * rest + row % rest)).astype(BF16)


def slot_keys(experts, rest, far, routes):
    tokens = routes.shape[1]
    names = iota((experts, tokens), 0)
    relative = [(routes[k : k + 1, :] + experts - far) % experts for k in range(2)]
    named = [(relative[k] == names).astype(F32) for k in range(2)]
    before = (iota((tokens, tokens), 0) < iota((tokens, tokens), 1)).astype(BF16)
    counts = dot((named[0] + named[1]).astype(BF16), before, ((1,), (0,)))
    keys = []
    for k in range(2):
        rank = jnp.sum(counts * named[k], axis=0, keepdims=True).astype(jnp.int32)
        keys.append(
            (
                jnp.where(rank < BASE, relative[k] * BASE + rank, -1),
                jnp.where(rank < BASE, -1, relative[k] * rest + rank - BASE),
            )
        )
    return keys


def exchange_kernel(
    experts, rest, fold, s_fold, chunks,
    routes_hbm, weights_hbm, rows_hbm, saved_hbm, w_hbm,
    pre_out, gate_out, down,
    routes, weights, rows, saved, w, pack, raw, names_in, relay_pick, relay, x_far, x, z,
    scaled, s_pack, s, s_wide, s_rest, s_turn, px_out, px_in, c_wide, c, r, c_routes,
    grad_gate_factor, grad_up_factor, plain, key_col, left_col, weight_col, gate_col, total,
    load_sem, tn, rn, tw, rw, tm, rm, tg, rg, tss, rss, tf, rf, tp, rp, tb, rb,
):
    d = lax.axis_index("dp")
    e = lax.axis_index("expert")
    other = 1 - d
    me = d * experts + e
    half_experts = experts // 2
    at = e % half_experts
    near = (e // half_experts) * half_experts
    far = half_experts - near
    quarter = half_experts // 2
    lane, plane = at % quarter, at // quarter
    capacity = BASE + rest
    wide = 2 * capacity
    slab = relay_pick.shape[1] // half_experts
    gateway = quarter * (1 + far // half_experts) + lane
    is_gateway = (e // quarter) % 3 != 0
    tokens, width = rows.shape
    half = width // 2
    part = half // fold
    hidden = w.shape[0]
    part_s = hidden // s_fold
    group = half_experts * BASE
    rest_group = half_experts * rest
    count = experts * BASE

    def block(i):
        return pl.ds(pl.multiple_of(i * BASE, BASE), BASE)

    def remote(src, dst, send, recv, to):
        return pltpu.make_async_remote_copy(
            src_ref=src, dst_ref=dst, send_sem=send, recv_sem=recv, device_id=to, device_id_type=MESH
        )

    def wait_bytes(ref, sem):
        pltpu.make_async_copy(ref, ref, sem).wait()

    def loop(first, last, body):
        def step(k, carry):
            body(k)
            return carry

        lax.fori_loop(first, last, step, 0)

    loads = [
        pltpu.make_async_copy(source, target, load_sem.at[i])
        for i, (source, target) in enumerate(
            (
                (routes_hbm, routes), (rows_hbm, rows), (weights_hbm, weights), (saved_hbm, saved),
                (w_hbm, w),
            )
        )
    ]
    for load in loads:
        load.start()
    barrier = pltpu.get_barrier_semaphore()

    def greet(k):
        p = (me + k) % (2 * experts)
        pl.semaphore_signal(
            barrier, inc=1, device_id=(p // experts, p % experts), device_id_type=MESH
        )

    loop(1, 2 * experts, greet)

    loads[0].wait()
    (key0, left0), (key1, left1) = slot_keys(experts, rest, far, routes[...])
    row = iota((group, tokens), 0)
    main_pick = ((key0 == row + group) | (key1 == row + group)).astype(BF16)
    slot = (row // BASE) * rest + row % rest + rest_group
    hit = (left0 == slot) | (left1 == slot)
    left_pick = jnp.concatenate(
        [(hit & ((row // rest) % fold == q)).astype(BF16) for q in range(fold)], axis=1
    )

    def columns_of(h, lo, size):
        return pl.ds(pl.multiple_of(h * half + lo, 128), size)

    def pack_half(side, h):
        for lo in range(0, half, 512):
            pack[side, :, lo : lo + 512] = dot(
                main_pick, rows[:, columns_of(h, lo, 512)], ((1,), (0,))
            ).astype(BF16)
        folded = jnp.concatenate([rows[:, columns_of(h, q * part, part)] for q in range(fold)], axis=0)
        pack[side, :, half : half + part] = dot(left_pick, folded, ((1,), (0,))).astype(BF16)

    def near_copy(side, j):
        return remote(
            pack.at[side, block(j)],
            x.at[block(side * half_experts + at)],
            tn.at[side],
            rn.at[side],
            (other if side == 0 else d, near + j),
        )

    chunk, ahead = half // chunks, 3

    def raw_copy(side, n):
        h = other if side == 0 else d
        return remote(
            rows.at[:, columns_of(h, n * chunk, chunk)],
            raw.at[side, pl.ds(pl.multiple_of(plane * tokens, tokens), tokens), n * chunk : (n + 1) * chunk],
            tw.at[side * chunks + n],
            rw.at[side * chunks + n],
            (h, gateway),
        )

    def names_copy(side):
        h = other if side == 0 else d
        return remote(routes, names_in.at[2 * side + plane], tm.at[0], rm.at[0], (h, gateway))

    loads[1].wait()
    pack_half(0, other)
    pack_half(1, d)
    pl.semaphore_wait(barrier, 2 * experts - 1)
    for side in range(2):
        names_copy(side).start()
    for n in range(ahead):
        for side in range(2):
            raw_copy(side, n).start()

    def each_near(body):
        for k in range(quarter):
            for p in range(2):
                j = (plane if p == 0 else 1 - plane) * quarter + (lane + k) % quarter
                body(j, k == 0 and p == 0)

    def start_near(j, is_self):
        near_copy(0, j).start()
        if not is_self:
            near_copy(1, j).start()

    each_near(start_near)
    pltpu.make_async_copy(
        pack.at[1, block(at)], x.at[block(half_experts + at)], rn.at[1]
    ).start()

    token_of = iota((2 * tokens, tokens), 0) // 2 == iota((2 * tokens, tokens), 1)
    first = iota((2 * tokens, tokens), 0) % 2 == 0

    def column(v0, v1):
        value = jnp.where(first, v0.astype(F32), v1.astype(F32))
        return jnp.sum(jnp.where(token_of, value, 0.0), axis=1, keepdims=True)

    loads[2].wait()
    key_col[...] = column(key0, key1).astype(jnp.int32)
    left_col[...] = column(left0, left1).astype(jnp.int32)
    weight_col[...] = column(weights[0:1, :], weights[1:2, :])
    loads[3].wait()
    step = 16

    @pl.loop(0, tokens // step)
    def _(i):
        mine = pl.ds(pl.multiple_of(i * 2 * step, 2 * step), 2 * step)
        both = saved[pl.ds(pl.multiple_of(i * step, step), step)].reshape(2 * step, 2 * hidden)
        gate_pre = both[:, :hidden].astype(F32)
        up_pre = both[:, hidden:].astype(F32)
        sigma = jax.nn.sigmoid(gate_pre)
        active = gate_pre * sigma
        weight = weight_col[mine, :]
        plain[mine, :] = (active * up_pre).astype(BF16)
        scaled[mine, :] = (weight * active * up_pre).astype(BF16)
        grad_up_factor[mine, :] = weight * active
        grad_gate_factor[mine, :] = weight * up_pre * sigma * (1.0 + gate_pre * (1.0 - sigma))

    slots = iota((2 * tokens, count), 1)

    def route_pick():
        return (key_col[...] == slots).astype(BF16)

    def route_left(q):
        wanted = (slots // BASE) * rest + slots % rest
        mine = (slots // rest) % fold == q
        return (mine & (left_col[...] == wanted)).astype(BF16)

    s_pack[:, 0:hidden] = dot(route_pick(), scaled[...], ((0,), (0,))).astype(BF16)
    folded = jnp.zeros((count, part_s), F32)
    for q in range(s_fold):
        folded = folded + dot(
            route_left(q), scaled[:, q * part_s : (q + 1) * part_s], ((0,), (0,))
        )
    s_pack[:, hidden : hidden + part_s] = folded.astype(BF16)

    def scaled_copy(is_far, j):
        g = 1 if is_far else 3
        n = 0 if is_far else 1
        source = s_pack.at[block(j if is_far else half_experts + j)]
        to = (d, (far if is_far else near) + j)
        return remote(source, s.at[block(g * half_experts + at)], tss.at[n], rss.at[n], to)

    def back_copy(is_far, j):
        n = 0 if is_far else 1
        source = c.at[block(j if is_far else half_experts + j)]
        to = (d, (far if is_far else near) + j)
        return remote(source, r.at[block(n * half_experts + at)], tb.at[n], rb.at[n], to)

    def rows_of(g):
        return slice(g * group, (g + 1) * group)

    def rest_of(g):
        return slice(g * rest_group, (g + 1) * rest_group)

    def slots_of(side):
        return slice(side * quarter * wide, (side + 1) * quarter * wide)

    def wide_pick(q, turned):
        shape = (quarter * wide, group) if turned else (group, quarter * wide)
        narrow, there = iota(shape, int(turned)), iota(shape, 1 - int(turned))
        source, inner = narrow // BASE, narrow % BASE
        base = (source % quarter) * wide + (source // quarter) * capacity
        if q is None:
            return (there == base + inner).astype(BF16)
        return ((there == base + BASE + inner % rest) & (inner // rest == q)).astype(BF16)

    def contract(n, side, put):
        if n == 0:
            lanes = slice(side * quarter, (side + 1) * quarter)
            wait_bytes(x_far.at[lanes], rg.at[side])
            lhs = x_far[lanes].reshape(quarter * wide, half)
        else:
            wait_bytes(x.at[rows_of(side)], rn.at[side])
            for q in range(fold):
                z[rest_of(side), q * part : (q + 1) * part] = dot(
                    unfold_pick(half_experts, rest, q),
                    x[rows_of(side), half : half + part],
                    ((1,), (0,)),
                ).astype(BF16)
            lhs = jnp.concatenate([x[rows_of(side), 0:half], z[rest_of(side), :]], axis=0)
        for lo in range(0, hidden, 256):
            put(lo, dot(lhs, w[lo : lo + 256, :], ((1,), (1,))))

    across = (other, e)

    def partial_copy(n):
        return remote(px_out.at[n], px_in.at[n], tp.at[n], rp.at[n], across)

    def forward_copy(n):
        g = 1 + 2 * n
        return remote(s.at[rows_of(g)], s.at[rows_of(g - 1)], tf.at[n], rf.at[n], across)

    loads[4].wait()

    def send_partial(n):
        def put(lo, value):
            px_out[n, :, lo : lo + 256] = value.astype(BF16)

        contract(n, 0, put)
        partial_copy(n).start()

    def finish(n):
        def put(lo, value):
            cut = slice(lo, lo + 256)
            summed = (value + px_in[n, :, cut].astype(F32)).astype(BF16)
            if n == 0:
                c_wide[:, cut] = summed
            else:
                c[rows_of(n), cut] = summed[:group]
                c_wide[0:rest_group, cut] = summed[group:]

        partial_copy(n).wait_recv()
        contract(n, 1, put)
        if n == 0:
            c[rows_of(n), 0:hidden] = dot(
                wide_pick(None, False), c_wide[...], ((1,), (0,))
            ).astype(BF16)
        folded = jnp.zeros((group, part_s), F32)
        for q in range(s_fold):
            cut = slice(q * part_s, (q + 1) * part_s)
            if n == 0:
                folded = folded + dot(wide_pick(q, False), c_wide[:, cut], ((1,), (0,)))
            else:
                folded = folded + dot(
                    fold_pick(half_experts, rest, fold, q), c_wide[0:rest_group, cut], ((1,), (0,))
                )
        c[rows_of(n), hidden : hidden + part_s] = folded.astype(BF16)

    def relay_copy(side, n, j):
        return remote(
            relay.at[side, n, j],
            x_far.at[side * quarter + lane, :, n * chunk : (n + 1) * chunk],
            tg.at[0],
            rg.at[side],
            (d, near + j),
        )

    def build_relay_pick():
        wait_bytes(names_in, rm.at[0])
        before = (iota((tokens, tokens), 0) < iota((tokens, tokens), 1)).astype(BF16)
        names = iota((half_experts, tokens), 0)
        target = iota((half_experts * slab, tokens), 0)
        for side in range(2):
            for p in range(2):
                named = [names_in[2 * side + p, k : k + 1, :] - near for k in range(2)]
                onehot = [(named[k] == names).astype(F32) for k in range(2)]
                counts = dot((onehot[0] + onehot[1]).astype(BF16), before, ((1,), (0,)))
                hits = []
                for k in range(2):
                    rank = jnp.sum(counts * onehot[k], axis=0, keepdims=True).astype(jnp.int32)
                    here = (named[k] >= 0) & (named[k] < half_experts)
                    hits.append(target == jnp.where(here, named[k] * slab + p * capacity + rank, -1))
                relay_pick[side, :, p * tokens : (p + 1) * tokens] = (hits[0] | hits[1]).astype(BF16)

    def relay_step(side, n):
        cut = slice(n * chunk, (n + 1) * chunk)
        wait_bytes(raw.at[side, :, cut], rw.at[side * chunks + n])
        packed = dot(relay_pick[side], raw[side, :, cut], ((1,), (0,))).astype(BF16)
        for j in range(half_experts):
            relay[side, n, j] = packed[j * slab : j * slab + wide]

        def start(j, is_self):
            if not is_self:
                relay_copy(side, n, j).start()

        each_near(start)
        pltpu.make_async_copy(
            relay.at[side, n, at],
            x_far.at[side * quarter + lane, :, cut],
            rg.at[side],
        ).start()

    def raw_steps(first, last):
        for n in range(first, last):

            @pl.when(is_gateway)
            def _():
                for side in range(2):
                    relay_step(side, n)

            for side in range(2):
                raw_copy(side, n).wait_send()
                if n + ahead < chunks:
                    raw_copy(side, n + ahead).start()

    def scaled_start(is_far):
        def start(k):
            scaled_copy(is_far, (at + k) % half_experts).start()

        loop(0 if is_far else 1, half_experts, start)

    pl.when(is_gateway)(build_relay_pick)
    raw_steps(0, chunks // 4)
    scaled_start(False)
    pltpu.make_async_copy(
        s_pack.at[block(half_experts + at)], s.at[block(3 * half_experts + at)], rss.at[1]
    ).start()
    raw_steps(chunks // 4, chunks // 2)
    send_partial(1)
    raw_steps(chunks // 2, 3 * chunks // 4)
    finish(1)

    def start_back_near(k):
        back_copy(False, (at + k) % half_experts).start()

    loop(1, half_experts, start_back_near)
    pltpu.make_async_copy(
        c.at[block(half_experts + at)], r.at[block(half_experts + at)], rb.at[1]
    ).start()
    wait_bytes(s.at[rows_of(3)], rss.at[1])
    forward_copy(1).start()

    raw_steps(3 * chunks // 4, chunks)
    scaled_start(True)
    send_partial(0)
    finish(0)

    def start_back_far(k):
        back_copy(True, (at + k) % half_experts).start()

    loop(0, half_experts, start_back_far)

    def turn(n):
        for side in range(2):
            g = 2 * n + side
            for q in range(s_fold):
                cut = slice(q * part_s, (q + 1) * part_s)
                tail = s[rows_of(g), hidden : hidden + part_s]
                if n == 0:
                    s_wide[slots_of(side), cut] = (
                        dot(wide_pick(None, True), s[rows_of(g), cut], ((1,), (0,)))
                        + dot(wide_pick(q, True), tail, ((1,), (0,)))
                    ).astype(BF16)
                else:
                    s_rest[rest_of(side), cut] = dot(
                        unfold_pick(half_experts, rest, q), tail, ((1,), (0,))
                    ).astype(BF16)
        if n == 0:
            s_turn[...] = s_wide[...].T
        else:
            s_turn[:, 0 : 2 * group] = s[2 * group : 4 * group, 0:hidden].T
            s_turn[:, 2 * group : 2 * group + 2 * rest_group] = s_rest[...].T

    def product(n, columns):
        if n == 0:
            rhs = x_far[:, :, columns].reshape(2 * quarter * wide, columns.size)
            return dot(s_turn[...], rhs, ((1,), (0,)))
        return dot(s_turn[:, 0 : 2 * group], x[:, columns], ((1,), (0,))) + dot(
            s_turn[:, 2 * group : 2 * group + 2 * rest_group], z[:, columns], ((1,), (0,))
        )

    forward_copy(1).wait_recv()
    turn(1)

    @pl.loop(0, half // 512)
    def _(j):
        columns = pl.ds(pl.multiple_of(j * 512, 512), 512)
        total[:, columns] = product(1, columns)

    wait_bytes(s.at[rows_of(1)], rss.at[0])
    forward_copy(0).start()
    forward_copy(0).wait_recv()
    turn(0)

    @pl.loop(0, half // 512)
    def _(j):
        columns = pl.ds(pl.multiple_of(j * 512, 512), 512)
        down[:, columns] = (total[:, columns] + product(0, columns)).astype(BF16)

    wait_bytes(r.at[rows_of(1)], rb.at[1])
    wait_bytes(r.at[rows_of(0)], rb.at[0])
    for q in range(s_fold):
        cut = slice(q * part_s, (q + 1) * part_s)
        c_routes[:, cut] = dot(route_pick(), r[:, cut], ((1,), (0,))) + dot(
            route_left(q), r[:, hidden : hidden + part_s], ((1,), (0,))
        )

    @pl.loop(0, tokens // step)
    def _(i):
        mine = pl.ds(pl.multiple_of(i * 2 * step, 2 * step), 2 * step)
        value = c_routes[mine, :]
        gate_col[mine, :] = jnp.sum(plain[mine, :].astype(F32) * value, axis=1, keepdims=True)
        out = jnp.concatenate(
            [value * grad_gate_factor[mine, :], value * grad_up_factor[mine, :]], axis=1
        ).astype(BF16)
        pre_out[pl.ds(pl.multiple_of(i * step, step), step)] = out.reshape(step, 2, 2 * hidden)

    for k in range(2):
        mine = token_of & (first if k == 0 else ~first)
        gate_out[k : k + 1, :] = jnp.sum(
            jnp.where(mine, gate_col[...], 0.0), axis=0, keepdims=True
        ).astype(BF16)

    wait_bytes(pack.at[0], tn.at[0])
    wait_bytes(pack.at[1, 0 : group - BASE], tn.at[1])
    wait_bytes(names_in.at[0:2], tm.at[0])

    @pl.when(is_gateway)
    def _():
        wait_bytes(relay.at[:, :, 0 : half_experts - 1], tg.at[0])

    wait_bytes(s_pack.at[0:group], tss.at[0])
    wait_bytes(s_pack.at[group : 2 * group - BASE], tss.at[1])
    wait_bytes(c.at[0:group], tb.at[0])
    wait_bytes(c.at[group : 2 * group - BASE], tb.at[1])
    for n in range(2):
        partial_copy(n).wait_send()
        forward_copy(n).wait_send()


def store_kernel(*refs):
    copies = [pltpu.make_async_copy(refs[i], refs[3 + i], refs[6].at[i]) for i in range(3)]
    for copy in copies:
        copy.start()
    for copy in copies:
        copy.wait()


def on_device(grad_out, saved_pre, gate_weight, routes, w_down):
    tokens, top_count = routes.shape
    hidden, half = w_down.shape[1:]
    width = grad_out.shape[1]
    experts = lax.axis_size("expert")
    replicas = lax.axis_size("dp")
    capacity = 5 * tokens * top_count // (4 * experts)
    if (replicas, top_count, experts, capacity, hidden, half % 512) != (2, 2, 16, 20, 768, 0):
        return on_device_general(grad_out, saved_pre, gate_weight, routes, w_down)
    rest = capacity - BASE
    fold = BASE // rest
    s_fold = hidden // 256
    devices = replicas * experts
    count, total = experts * BASE, devices * BASE
    part, part_s = half // fold, hidden // s_fold
    finished = (count + experts * rest) // 2
    chunks = half // 256
    vmem = pl.BlockSpec(memory_space=pltpu.VMEM)
    stored = pl.BlockSpec(memory_space=pltpu.HBM)
    dma = pltpu.SemaphoreType.DMA
    pre, gate, down = pl.pallas_call(
        functools.partial(exchange_kernel, experts, rest, fold, s_fold, chunks),
        out_shape=(
            pltpu.VMEM(saved_pre.shape, BF16),
            pltpu.VMEM((top_count, tokens), BF16),
            pltpu.VMEM((hidden, half), BF16),
        ),
        in_specs=[stored] * 5,
        out_specs=[vmem] * 3,
        scratch_shapes=[
            pltpu.VMEM((top_count, tokens), jnp.int32),
            pltpu.VMEM((top_count, tokens), BF16),
            pltpu.VMEM((tokens, width), BF16),
            pltpu.VMEM(saved_pre.shape, BF16),
            pltpu.VMEM((hidden, half), BF16),
            pltpu.VMEM((2, count // 2, half + part), BF16),
            pltpu.VMEM((2, 2 * tokens, half), BF16),
            pltpu.VMEM((4, top_count, tokens), jnp.int32),
            pltpu.VMEM((2, experts // 2 * -(-2 * capacity // 16) * 16, 2 * tokens), BF16),
            pltpu.VMEM((2, chunks, experts // 2, 2 * capacity, half // chunks), BF16),
            pltpu.VMEM((experts // 2, 2 * capacity, half), BF16),
            pltpu.VMEM((count, half + part), BF16),
            pltpu.VMEM((experts * rest, half), BF16),
            pltpu.VMEM((2 * tokens, hidden), BF16),
            pltpu.VMEM((count, hidden + part_s), BF16),
            pltpu.VMEM((total, hidden + part_s), BF16),
            pltpu.VMEM((2 * finished, hidden), BF16),
            pltpu.VMEM((experts * rest, hidden), BF16),
            pltpu.VMEM((hidden, 2 * finished), BF16),
            pltpu.VMEM((2, finished, hidden), BF16),
            pltpu.VMEM((2, finished, hidden), BF16),
            pltpu.VMEM((finished, hidden), BF16),
            pltpu.VMEM((count, hidden + part_s), BF16),
            pltpu.VMEM((count, hidden + part_s), BF16),
            pltpu.VMEM((2 * tokens, hidden), F32),
            pltpu.VMEM((2 * tokens, hidden), F32),
            pltpu.VMEM((2 * tokens, hidden), F32),
            pltpu.VMEM((2 * tokens, hidden), BF16),
            pltpu.VMEM((2 * tokens, 1), jnp.int32),
            pltpu.VMEM((2 * tokens, 1), jnp.int32),
            pltpu.VMEM((2 * tokens, 1), F32),
            pltpu.VMEM((2 * tokens, 1), F32),
            pltpu.VMEM((hidden, half), F32),
            dma((5,)),
            dma((2,)), dma((2,)), dma((2 * chunks,)), dma((2 * chunks,)), dma((1,)), dma((1,)),
            dma((1,)), dma((2,)),
            dma((2,)), dma((2,)), dma((2,)), dma((2,)),
            dma((2,)), dma((2,)), dma((2,)), dma((2,)),
        ],
        compiler_params=pltpu.CompilerParams(
            collective_id=0, has_side_effects=True, vmem_limit_bytes=40 << 20
        ),
    )(*[
        pltpu.with_memory_space_constraint(operand, pltpu.HBM)
        for operand in (routes.T, gate_weight.T, grad_out, saved_pre, w_down[0])
    ])
    pre, gate, down = pl.pallas_call(
        store_kernel,
        out_shape=[jax.ShapeDtypeStruct(a.shape, a.dtype) for a in (pre, gate, down)],
        in_specs=[vmem] * 3,
        out_specs=[stored] * 3,
        scratch_shapes=[dma((3,))],
        compiler_params=pltpu.CompilerParams(vmem_limit_bytes=1 << 20),
    )(pre, gate, down)
    return pre, gate.T, down[None]


def solution(mesh):
    return jax.shard_map(
        on_device,
        mesh=mesh,
        in_specs=(
            P(("dp", "expert"), None),
            P(("dp", "expert"), None, None),
            P(("dp", "expert"), None),
            P(("dp", "expert"), None),
            P("expert", None, "dp"),
        ),
        out_specs=(
            P(("dp", "expert"), None, None),
            P(("dp", "expert"), None),
            P("expert", None, "dp"),
        ),
        check_vma=False,
    )
```

```python
import functools

import jax
import jax.numpy as jnp
from jax import lax
from jax.experimental import pallas as pl
from jax.experimental.pallas import tpu as pltpu
from jax.sharding import PartitionSpec as P

BF16 = jnp.bfloat16
F32 = jnp.float32


def slot_positions(routes_flat, experts, capacity):
    expert_ids = jnp.arange(experts, dtype=jnp.int32)
    onehot = (routes_flat[:, None] == expert_ids[None, :]).astype(BF16)
    ids = jnp.arange(routes_flat.shape[0], dtype=jnp.int32)
    before = (ids[None, :] < ids[:, None]).astype(BF16)
    counts = dot(before, onehot, ((1,), (0,)))
    rank = jnp.sum(counts * onehot.astype(F32), axis=1).astype(jnp.int32)
    return routes_flat * capacity + rank


def swiglu_parts(saved, hidden):
    gate_pre = saved[..., :hidden].astype(F32)
    up_pre = saved[..., hidden:].astype(F32)
    return (gate_pre, up_pre, jax.nn.silu(gate_pre))


def swiglu_grads(saved, weights, contraction, hidden):
    gate_pre, up_pre, active = swiglu_parts(saved, hidden)
    plain = (active * up_pre).astype(BF16)
    gate_grad = jnp.sum(plain.astype(F32) * contraction.astype(F32), axis=-1).astype(BF16)
    back = weights.astype(F32)[..., None] * contraction.astype(F32)
    sigma = jax.nn.sigmoid(gate_pre)
    grad_gate_pre = back * up_pre * sigma * (1.0 + gate_pre * (1.0 - sigma))
    grad_up_pre = back * active
    return (jnp.concatenate([grad_gate_pre, grad_up_pre], axis=-1).astype(BF16), gate_grad)


def scaled_hidden(saved, weights, hidden):
    gate_pre, up_pre, active = swiglu_parts(saved, hidden)
    return (weights.astype(F32)[..., None] * active * up_pre).astype(BF16)


def dot(a, b, dims):
    return lax.dot_general(a, b, (dims, ((), ())), preferred_element_type=F32)


def on_device_general(grad_out, saved_pre, gate_weight, routes, w_down):
    tokens_dev, top_count = routes.shape
    hidden = w_down.shape[1]
    half = w_down.shape[2]
    experts = lax.axis_size("expert")
    replicas = lax.axis_size("dp")
    capacity = 5 * tokens_dev * top_count // (4 * experts)
    slots = experts * capacity
    positions = slot_positions(routes.reshape(-1), experts, capacity).reshape(tokens_dev, top_count)
    slot_ids = jnp.arange(slots, dtype=jnp.int32)
    picks = [
        (positions[:, k][None, :] == slot_ids[:, None]).astype(BF16) for k in range(top_count)
    ]
    pick = sum(picks[1:], picks[0])
    devices = replicas * experts
    send_rows = jnp.stack(
        [
            dot(pick, grad_out[:, d * half : (d + 1) * half], ((1,), (0,))).astype(BF16)
            for d in range(replicas)
        ]
    ).reshape(devices, capacity, half)
    scaled = scaled_hidden(saved_pre, gate_weight, hidden)
    send_scaled = sum(dot(picks[k], scaled[:, k], ((1,), (0,))) for k in range(top_count))
    send_scaled = send_scaled.astype(BF16).reshape(experts, capacity, hidden)
    rows = lax.all_to_all(send_rows, ("dp", "expert"), split_axis=0, concat_axis=0, tiled=True)
    scaled_in = lax.all_to_all(send_scaled, "expert", split_axis=0, concat_axis=0, tiled=True)
    scaled_in = lax.all_gather(scaled_in.reshape(slots, hidden), "dp", axis=0, tiled=True)
    rows = rows.reshape(devices * capacity, half)
    partial = dot(rows, w_down[0], ((1,), (1,))).astype(BF16).reshape(devices, capacity, hidden)
    parts = lax.all_to_all(partial, ("dp", "expert"), split_axis=0, concat_axis=0, tiled=True)
    parts = parts.reshape(replicas, slots, hidden)
    contraction = jnp.stack(
        [
            sum(dot(picks[k], parts[d], ((0,), (0,))) for d in range(replicas))
            for k in range(top_count)
        ],
        axis=1,
    ).astype(BF16)
    grads, gate_grad = swiglu_grads(saved_pre, gate_weight, contraction, hidden)
    grad_down = dot(scaled_in, rows, ((0,), (0,))).astype(BF16)
    return grads, gate_grad, grad_down[None]


BASE = 16
MESH = pl.DeviceIdType.MESH


def iota(shape, axis):
    return lax.broadcasted_iota(jnp.int32, shape, axis)


def unfold_pick(groups, rest, q):
    shape = (groups * rest, groups * BASE)
    row, col = iota(shape, 0), iota(shape, 1)
    return (col == (row // rest) * BASE + q * rest + row % rest).astype(BF16)


def fold_pick(groups, rest, fold, q):
    shape = (groups * BASE, groups * rest)
    row, col = iota(shape, 0), iota(shape, 1)
    mine = (row // rest) % fold == q
    return (mine & (col == (row // BASE) * rest + row % rest)).astype(BF16)


def slot_keys(experts, rest, far, routes):
    tokens = routes.shape[1]
    names = iota((experts, tokens), 0)
    relative = [(routes[k : k + 1, :] + experts - far) % experts for k in range(2)]
    named = [(relative[k] == names).astype(F32) for k in range(2)]
    before = (iota((tokens, tokens), 0) < iota((tokens, tokens), 1)).astype(BF16)
    counts = dot((named[0] + named[1]).astype(BF16), before, ((1,), (0,)))
    keys = []
    for k in range(2):
        rank = jnp.sum(counts * named[k], axis=0, keepdims=True).astype(jnp.int32)
        keys.append(
            (
                jnp.where(rank < BASE, relative[k] * BASE + rank, -1),
                jnp.where(rank < BASE, -1, relative[k] * rest + rank - BASE),
            )
        )
    return keys


def exchange_kernel(
    experts, rest, fold, s_fold, chunks,
    routes_hbm, weights_hbm, rows_hbm, saved_hbm, w_hbm,
    pre_out, gate_out, down,
    routes, weights, rows, saved, w, pack, raw, names_in, relay_pick, relay, x_far, x, z,
    scaled, s_pack, s, s_wide, s_rest, s_turn, s_far, px_out, px_in, c_wide, c, r, c_routes,
    grad_gate_factor, grad_up_factor, plain, key_col, left_col, weight_col, gate_col, total,
    load_sem, tn, rn, tw, rw, tm, rm, tg, rg, tss, rss, tf, rf, tp, rp, tb, rb,
):
    d = lax.axis_index("dp")
    e = lax.axis_index("expert")
    other = 1 - d
    me = d * experts + e
    half_experts = experts // 2
    at = e % half_experts
    near = (e // half_experts) * half_experts
    far = half_experts - near
    quarter = half_experts // 2
    lane, plane = at % quarter, at // quarter
    capacity = BASE + rest
    wide = 2 * capacity
    slab = relay_pick.shape[1] // half_experts
    gateway = quarter * (1 + far // half_experts) + lane
    is_gateway = (e // quarter) % 3 != 0
    tokens, width = rows.shape
    half = width // 2
    part = half // fold
    hidden = w.shape[0]
    part_s = hidden // s_fold
    group = half_experts * BASE
    rest_group = half_experts * rest
    count = experts * BASE

    def block(i):
        return pl.ds(pl.multiple_of(i * BASE, BASE), BASE)

    def remote(src, dst, send, recv, to):
        return pltpu.make_async_remote_copy(
            src_ref=src, dst_ref=dst, send_sem=send, recv_sem=recv, device_id=to, device_id_type=MESH
        )

    def wait_bytes(ref, sem):
        pltpu.make_async_copy(ref, ref, sem).wait()

    def loop(first, last, body):
        def step(k, carry):
            body(k)
            return carry

        lax.fori_loop(first, last, step, 0)

    loads = [
        pltpu.make_async_copy(source, target, load_sem.at[i])
        for i, (source, target) in enumerate(
            (
                (routes_hbm, routes), (rows_hbm, rows), (weights_hbm, weights), (saved_hbm, saved),
                (w_hbm, w),
            )
        )
    ]
    for load in loads:
        load.start()
    barrier = pltpu.get_barrier_semaphore()

    def greet(k):
        p = (me + k) % (2 * experts)
        pl.semaphore_signal(
            barrier, inc=1, device_id=(p // experts, p % experts), device_id_type=MESH
        )

    loop(1, 2 * experts, greet)

    loads[0].wait()
    (key0, left0), (key1, left1) = slot_keys(experts, rest, far, routes[...])
    row = iota((group, tokens), 0)
    main_pick = ((key0 == row + group) | (key1 == row + group)).astype(BF16)
    slot = (row // BASE) * rest + row % rest + rest_group
    hit = (left0 == slot) | (left1 == slot)
    left_pick = jnp.concatenate(
        [(hit & ((row // rest) % fold == q)).astype(BF16) for q in range(fold)], axis=1
    )

    def columns_of(h, lo, size):
        return pl.ds(pl.multiple_of(h * half + lo, 128), size)

    def pack_half(side, h):
        for lo in range(0, half, 512):
            pack[side, :, lo : lo + 512] = dot(
                main_pick, rows[:, columns_of(h, lo, 512)], ((1,), (0,))
            ).astype(BF16)
        folded = jnp.concatenate([rows[:, columns_of(h, q * part, part)] for q in range(fold)], axis=0)
        pack[side, :, half : half + part] = dot(left_pick, folded, ((1,), (0,))).astype(BF16)

    def near_copy(side, j):
        return remote(
            pack.at[side, block(j)],
            x.at[block(side * half_experts + at)],
            tn.at[side],
            rn.at[side],
            (other if side == 0 else d, near + j),
        )

    chunk, ahead, lead = half // chunks, 8, 3
    order = [(0, n) for n in range(lead)]
    for n in range(chunks):
        order += [(0, n + lead)] * (n + lead < chunks) + [(1, n)]

    def raw_copy(side, n):
        h = other if side == 0 else d
        return remote(
            rows.at[:, columns_of(h, n * chunk, chunk)],
            raw.at[side, pl.ds(pl.multiple_of(plane * tokens, tokens), tokens), n * chunk : (n + 1) * chunk],
            tw.at[side * chunks + n],
            rw.at[side * chunks + n],
            (h, gateway),
        )

    def names_copy(side):
        h = other if side == 0 else d
        return remote(routes, names_in.at[2 * side + plane], tm.at[0], rm.at[0], (h, gateway))

    loads[1].wait()
    pack_half(0, other)
    pack_half(1, d)
    pl.semaphore_wait(barrier, 2 * experts - 1)
    for side in range(2):
        names_copy(side).start()
    for side, n in order[:ahead]:
        raw_copy(side, n).start()

    def each_near(body):
        for k in range(quarter):
            for p in range(2):
                j = (plane if p == 0 else 1 - plane) * quarter + (lane + k) % quarter
                body(j, k == 0 and p == 0)

    def start_near_own(j, is_self):
        if not is_self:
            near_copy(1, j).start()

    def start_near_across(j, is_self):
        near_copy(0, j).start()

    each_near(start_near_own)
    pltpu.make_async_copy(
        pack.at[1, block(at)], x.at[block(half_experts + at)], rn.at[1]
    ).start()

    token_of = iota((2 * tokens, tokens), 0) // 2 == iota((2 * tokens, tokens), 1)
    first = iota((2 * tokens, tokens), 0) % 2 == 0

    def column(v0, v1):
        value = jnp.where(first, v0.astype(F32), v1.astype(F32))
        return jnp.sum(jnp.where(token_of, value, 0.0), axis=1, keepdims=True)

    loads[2].wait()
    key_col[...] = column(key0, key1).astype(jnp.int32)
    left_col[...] = column(left0, left1).astype(jnp.int32)
    weight_col[...] = column(weights[0:1, :], weights[1:2, :])
    loads[3].wait()
    step = 16

    @pl.loop(0, tokens // step)
    def _(i):
        mine = pl.ds(pl.multiple_of(i * 2 * step, 2 * step), 2 * step)
        both = saved[pl.ds(pl.multiple_of(i * step, step), step)].reshape(2 * step, 2 * hidden)
        gate_pre = both[:, :hidden].astype(F32)
        up_pre = both[:, hidden:].astype(F32)
        sigma = jax.nn.sigmoid(gate_pre)
        active = gate_pre * sigma
        weight = weight_col[mine, :]
        plain[mine, :] = (active * up_pre).astype(BF16)
        scaled[mine, :] = (weight * active * up_pre).astype(BF16)
        grad_up_factor[mine, :] = weight * active
        grad_gate_factor[mine, :] = weight * up_pre * sigma * (1.0 + gate_pre * (1.0 - sigma))

    slots = iota((2 * tokens, count), 1)

    def route_pick():
        return (key_col[...] == slots).astype(BF16)

    def route_left(q):
        wanted = (slots // BASE) * rest + slots % rest
        mine = (slots // rest) % fold == q
        return (mine & (left_col[...] == wanted)).astype(BF16)

    s_pack[:, 0:hidden] = dot(route_pick(), scaled[...], ((0,), (0,))).astype(BF16)
    folded = jnp.zeros((count, part_s), F32)
    for q in range(s_fold):
        folded = folded + dot(
            route_left(q), scaled[:, q * part_s : (q + 1) * part_s], ((0,), (0,))
        )
    s_pack[:, hidden : hidden + part_s] = folded.astype(BF16)

    def scaled_copy(is_far, j):
        g = 1 if is_far else 3
        n = 1 + at if is_far else 0
        source = s_pack.at[block(j if is_far else half_experts + j)]
        to = (d, (far if is_far else near) + j)
        return remote(source, s.at[block(g * half_experts + at)], tss.at[int(is_far)], rss.at[n], to)

    def back_copy(is_far, j):
        n = 0 if is_far else 1
        source = c.at[block(j if is_far else half_experts + j)]
        to = (d, (far if is_far else near) + j)
        return remote(source, r.at[block(n * half_experts + at)], tb.at[n], rb.at[n], to)

    def rows_of(g):
        return slice(g * group, (g + 1) * group)

    def rest_of(g):
        return slice(g * rest_group, (g + 1) * rest_group)

    def slots_of(side):
        return slice(side * quarter * wide, (side + 1) * quarter * wide)

    def wide_pick(q, turned):
        shape = (quarter * wide, group) if turned else (group, quarter * wide)
        narrow, there = iota(shape, int(turned)), iota(shape, 1 - int(turned))
        source, inner = narrow // BASE, narrow % BASE
        base = (source % quarter) * wide + (source // quarter) * capacity
        if q is None:
            return (there == base + inner).astype(BF16)
        return ((there == base + BASE + inner % rest) & (inner // rest == q)).astype(BF16)

    def contract(n, side, put):
        if n == 0:
            lanes = slice(side * quarter, (side + 1) * quarter)
            wait_bytes(x_far.at[lanes], rg.at[side])
            lhs = x_far[lanes].reshape(quarter * wide, half)
        else:
            wait_bytes(x.at[rows_of(side)], rn.at[side])
            for q in range(fold):
                z[rest_of(side), q * part : (q + 1) * part] = dot(
                    unfold_pick(half_experts, rest, q),
                    x[rows_of(side), half : half + part],
                    ((1,), (0,)),
                ).astype(BF16)
            lhs = jnp.concatenate([x[rows_of(side), 0:half], z[rest_of(side), :]], axis=0)
        for lo in range(0, hidden, 256):
            put(lo, dot(lhs, w[lo : lo + 256, :], ((1,), (1,))))

    across = (other, e)

    def partial_copy(n):
        return remote(px_out.at[n], px_in.at[n], tp.at[n], rp.at[n], across)

    def forward_near():
        return remote(s.at[rows_of(3)], s.at[rows_of(2)], tf.at[0], rf.at[0], across)

    def forward_far(j):
        return remote(
            s.at[block(half_experts + j)], s.at[block(j)], tf.at[1 + j], rf.at[1 + j], across
        )

    loads[4].wait()

    def send_partial(n):
        def put(lo, value):
            px_out[n, :, lo : lo + 256] = value.astype(BF16)

        contract(n, 0, put)
        partial_copy(n).start()

    def finish(n):
        def put(lo, value):
            cut = slice(lo, lo + 256)
            summed = (value + px_in[n, :, cut].astype(F32)).astype(BF16)
            if n == 0:
                c_wide[:, cut] = summed
            else:
                c[rows_of(n), cut] = summed[:group]
                c_wide[0:rest_group, cut] = summed[group:]

        partial_copy(n).wait_recv()
        contract(n, 1, put)
        if n == 0:
            c[rows_of(n), 0:hidden] = dot(
                wide_pick(None, False), c_wide[...], ((1,), (0,))
            ).astype(BF16)
        folded = jnp.zeros((group, part_s), F32)
        for q in range(s_fold):
            cut = slice(q * part_s, (q + 1) * part_s)
            if n == 0:
                folded = folded + dot(wide_pick(q, False), c_wide[:, cut], ((1,), (0,)))
            else:
                folded = folded + dot(
                    fold_pick(half_experts, rest, fold, q), c_wide[0:rest_group, cut], ((1,), (0,))
                )
        c[rows_of(n), hidden : hidden + part_s] = folded.astype(BF16)

    def relay_copy(side, n, j):
        return remote(
            relay.at[side, n, j],
            x_far.at[side * quarter + lane, :, n * chunk : (n + 1) * chunk],
            tg.at[0],
            rg.at[side],
            (d, near + j),
        )

    def build_relay_pick():
        wait_bytes(names_in, rm.at[0])
        before = (iota((tokens, tokens), 0) < iota((tokens, tokens), 1)).astype(BF16)
        names = iota((half_experts, tokens), 0)
        target = iota((half_experts * slab, tokens), 0)
        for side in range(2):
            for p in range(2):
                named = [names_in[2 * side + p, k : k + 1, :] - near for k in range(2)]
                onehot = [(named[k] == names).astype(F32) for k in range(2)]
                counts = dot((onehot[0] + onehot[1]).astype(BF16), before, ((1,), (0,)))
                hits = []
                for k in range(2):
                    rank = jnp.sum(counts * onehot[k], axis=0, keepdims=True).astype(jnp.int32)
                    here = (named[k] >= 0) & (named[k] < half_experts)
                    hits.append(target == jnp.where(here, named[k] * slab + p * capacity + rank, -1))
                relay_pick[side, :, p * tokens : (p + 1) * tokens] = (hits[0] | hits[1]).astype(BF16)

    def relay_step(side, n):
        cut = slice(n * chunk, (n + 1) * chunk)
        wait_bytes(raw.at[side, :, cut], rw.at[side * chunks + n])
        packed = dot(relay_pick[side], raw[side, :, cut], ((1,), (0,))).astype(BF16)
        for j in range(half_experts):
            relay[side, n, j] = packed[j * slab : j * slab + wide]

        def start(j, is_self):
            if not is_self:
                relay_copy(side, n, j).start()

        each_near(start)
        pltpu.make_async_copy(
            relay.at[side, n, at],
            x_far.at[side * quarter + lane, :, cut],
            rg.at[side],
        ).start()

    def raw_steps(first, last):
        for i in range(first, last):

            @pl.when(is_gateway)
            def _():
                relay_step(*order[i])

            raw_copy(*order[i]).wait_send()
            if i + ahead < len(order):
                raw_copy(*order[i + ahead]).start()

    def scaled_start(is_far):
        def start(k):
            scaled_copy(is_far, (at + k) % half_experts).start()

        loop(0 if is_far else 1, half_experts, start)

    pl.when(is_gateway)(build_relay_pick)
    each_near(start_near_across)
    raw_steps(0, 4)
    scaled_start(False)
    pltpu.make_async_copy(
        s_pack.at[block(half_experts + at)], s.at[block(3 * half_experts + at)], rss.at[0]
    ).start()
    raw_steps(4, 10)
    wait_bytes(s.at[rows_of(3)], rss.at[0])
    forward_near().start()
    send_partial(1)
    raw_steps(10, 14)
    send_partial(0)
    raw_steps(14, 16)
    scaled_start(True)
    finish(0)
    def start_back_far(k):
        back_copy(True, (at + k) % half_experts).start()

    loop(0, half_experts, start_back_far)

    finish(1)
    def start_back_near(k):
        back_copy(False, (at + k) % half_experts).start()

    loop(1, half_experts, start_back_near)
    pltpu.make_async_copy(
        c.at[block(half_experts + at)], r.at[block(half_experts + at)], rb.at[1]
    ).start()


    def widen(side):
        for q in range(s_fold):
            cut = slice(q * part_s, (q + 1) * part_s)
            s_wide[slots_of(side), cut] = (
                dot(wide_pick(None, True), s[rows_of(side), cut], ((1,), (0,)))
                + dot(wide_pick(q, True), s[rows_of(side), hidden : hidden + part_s], ((1,), (0,)))
            ).astype(BF16)

    def turn_near():
        for side in range(2):
            for q in range(s_fold):
                s_rest[rest_of(side), q * part_s : (q + 1) * part_s] = dot(
                    unfold_pick(half_experts, rest, q),
                    s[rows_of(2 + side), hidden : hidden + part_s],
                    ((1,), (0,)),
                ).astype(BF16)
        s_turn[:, 0 : 2 * group] = s[2 * group : 4 * group, 0:hidden].T
        s_turn[:, 2 * group : 2 * group + 2 * rest_group] = s_rest[...].T

    def near_product(columns):
        return dot(s_turn[:, 0 : 2 * group], x[:, columns], ((1,), (0,))) + dot(
            s_turn[:, 2 * group : 2 * group + 2 * rest_group], z[:, columns], ((1,), (0,))
        )

    def far_product(side, columns):
        rhs = x_far[side * quarter : (side + 1) * quarter, :, columns]
        return dot(s_far[side], rhs.reshape(quarter * wide, columns.size), ((1,), (0,)))

    def each_columns(body):
        @pl.loop(0, half // 512)
        def _(j):
            body(pl.ds(pl.multiple_of(j * 512, 512), 512))

    forward_near().wait_recv()
    turn_near()

    def add_near(columns):
        total[:, columns] = near_product(columns)

    each_columns(add_near)

    def pass_on(k):
        j = (at + half_experts - k) % half_experts
        wait_bytes(s.at[block(half_experts + j)], rss.at[1 + j])
        forward_far(j).start()

    loop(0, half_experts, pass_on)
    widen(1)
    s_far[1] = s_wide[slots_of(1), :].T

    def add_own(columns):
        total[:, columns] = total[:, columns] + far_product(1, columns)

    each_columns(add_own)
    loop(0, half_experts, lambda j: forward_far(j).wait_recv())
    widen(0)
    s_far[0] = s_wide[slots_of(0), :].T

    def add_across(columns):
        down[:, columns] = (total[:, columns] + far_product(0, columns)).astype(BF16)

    each_columns(add_across)

    wait_bytes(r.at[rows_of(1)], rb.at[1])
    wait_bytes(r.at[rows_of(0)], rb.at[0])
    for q in range(s_fold):
        cut = slice(q * part_s, (q + 1) * part_s)
        c_routes[:, cut] = dot(route_pick(), r[:, cut], ((1,), (0,))) + dot(
            route_left(q), r[:, hidden : hidden + part_s], ((1,), (0,))
        )

    @pl.loop(0, tokens // step)
    def _(i):
        mine = pl.ds(pl.multiple_of(i * 2 * step, 2 * step), 2 * step)
        value = c_routes[mine, :]
        gate_col[mine, :] = jnp.sum(plain[mine, :].astype(F32) * value, axis=1, keepdims=True)
        out = jnp.concatenate(
            [value * grad_gate_factor[mine, :], value * grad_up_factor[mine, :]], axis=1
        ).astype(BF16)
        pre_out[pl.ds(pl.multiple_of(i * step, step), step)] = out.reshape(step, 2, 2 * hidden)

    for k in range(2):
        mine = token_of & (first if k == 0 else ~first)
        gate_out[k : k + 1, :] = jnp.sum(
            jnp.where(mine, gate_col[...], 0.0), axis=0, keepdims=True
        ).astype(BF16)

    wait_bytes(pack.at[0], tn.at[0])
    wait_bytes(pack.at[1, 0 : group - BASE], tn.at[1])
    wait_bytes(names_in.at[0:2], tm.at[0])

    @pl.when(is_gateway)
    def _():
        wait_bytes(relay.at[:, :, 0 : half_experts - 1], tg.at[0])

    wait_bytes(s_pack.at[0:group], tss.at[1])
    wait_bytes(s_pack.at[group : 2 * group - BASE], tss.at[0])
    wait_bytes(c.at[0:group], tb.at[0])
    wait_bytes(c.at[group : 2 * group - BASE], tb.at[1])
    for n in range(2):
        partial_copy(n).wait_send()
    forward_near().wait_send()
    loop(0, half_experts, lambda j: forward_far(j).wait_send())


def store_kernel(*refs):
    copies = [pltpu.make_async_copy(refs[i], refs[3 + i], refs[6].at[i]) for i in range(3)]
    for copy in copies:
        copy.start()
    for copy in copies:
        copy.wait()


def on_device(grad_out, saved_pre, gate_weight, routes, w_down):
    tokens, top_count = routes.shape
    hidden, half = w_down.shape[1:]
    width = grad_out.shape[1]
    experts = lax.axis_size("expert")
    replicas = lax.axis_size("dp")
    capacity = 5 * tokens * top_count // (4 * experts)
    if (replicas, top_count, experts, capacity, hidden, half % 512) != (2, 2, 16, 20, 768, 0):
        return on_device_general(grad_out, saved_pre, gate_weight, routes, w_down)
    rest = capacity - BASE
    fold = BASE // rest
    s_fold = hidden // 256
    devices = replicas * experts
    count, total = experts * BASE, devices * BASE
    part, part_s = half // fold, hidden // s_fold
    finished = (count + experts * rest) // 2
    chunks = half // 256
    vmem = pl.BlockSpec(memory_space=pltpu.VMEM)
    stored = pl.BlockSpec(memory_space=pltpu.HBM)
    dma = pltpu.SemaphoreType.DMA
    pre, gate, down = pl.pallas_call(
        functools.partial(exchange_kernel, experts, rest, fold, s_fold, chunks),
        out_shape=(
            pltpu.VMEM(saved_pre.shape, BF16),
            pltpu.VMEM((top_count, tokens), BF16),
            pltpu.VMEM((hidden, half), BF16),
        ),
        in_specs=[stored] * 5,
        out_specs=[vmem] * 3,
        scratch_shapes=[
            pltpu.VMEM((top_count, tokens), jnp.int32),
            pltpu.VMEM((top_count, tokens), BF16),
            pltpu.VMEM((tokens, width), BF16),
            pltpu.VMEM(saved_pre.shape, BF16),
            pltpu.VMEM((hidden, half), BF16),
            pltpu.VMEM((2, count // 2, half + part), BF16),
            pltpu.VMEM((2, 2 * tokens, half), BF16),
            pltpu.VMEM((4, top_count, tokens), jnp.int32),
            pltpu.VMEM((2, experts // 2 * -(-2 * capacity // 16) * 16, 2 * tokens), BF16),
            pltpu.VMEM((2, chunks, experts // 2, 2 * capacity, half // chunks), BF16),
            pltpu.VMEM((experts // 2, 2 * capacity, half), BF16),
            pltpu.VMEM((count, half + part), BF16),
            pltpu.VMEM((experts * rest, half), BF16),
            pltpu.VMEM((2 * tokens, hidden), BF16),
            pltpu.VMEM((count, hidden + part_s), BF16),
            pltpu.VMEM((total, hidden + part_s), BF16),
            pltpu.VMEM((2 * finished, hidden), BF16),
            pltpu.VMEM((experts * rest, hidden), BF16),
            pltpu.VMEM((hidden, 2 * finished), BF16),
            pltpu.VMEM((2, hidden, finished), BF16),
            pltpu.VMEM((2, finished, hidden), BF16),
            pltpu.VMEM((2, finished, hidden), BF16),
            pltpu.VMEM((finished, hidden), BF16),
            pltpu.VMEM((count, hidden + part_s), BF16),
            pltpu.VMEM((count, hidden + part_s), BF16),
            pltpu.VMEM((2 * tokens, hidden), F32),
            pltpu.VMEM((2 * tokens, hidden), F32),
            pltpu.VMEM((2 * tokens, hidden), F32),
            pltpu.VMEM((2 * tokens, hidden), BF16),
            pltpu.VMEM((2 * tokens, 1), jnp.int32),
            pltpu.VMEM((2 * tokens, 1), jnp.int32),
            pltpu.VMEM((2 * tokens, 1), F32),
            pltpu.VMEM((2 * tokens, 1), F32),
            pltpu.VMEM((hidden, half), F32),
            dma((5,)),
            dma((2,)), dma((2,)), dma((2 * chunks,)), dma((2 * chunks,)), dma((1,)), dma((1,)),
            dma((1,)), dma((2,)),
            dma((2,)), dma((experts,)), dma((experts,)), dma((experts,)),
            dma((2,)), dma((2,)), dma((2,)), dma((2,)),
        ],
        compiler_params=pltpu.CompilerParams(
            collective_id=0, has_side_effects=True, vmem_limit_bytes=40 << 20
        ),
    )(*[
        pltpu.with_memory_space_constraint(operand, pltpu.HBM)
        for operand in (routes.T, gate_weight.T, grad_out, saved_pre, w_down[0])
    ])
    pre, gate, down = pl.pallas_call(
        store_kernel,
        out_shape=[jax.ShapeDtypeStruct(a.shape, a.dtype) for a in (pre, gate, down)],
        in_specs=[vmem] * 3,
        out_specs=[stored] * 3,
        scratch_shapes=[dma((3,))],
        compiler_params=pltpu.CompilerParams(vmem_limit_bytes=1 << 20),
    )(pre, gate, down)
    return pre, gate.T, down[None]


def solution(mesh):
    return jax.shard_map(
        on_device,
        mesh=mesh,
        in_specs=(
            P(("dp", "expert"), None),
            P(("dp", "expert"), None, None),
            P(("dp", "expert"), None),
            P(("dp", "expert"), None),
            P("expert", None, "dp"),
        ),
        out_specs=(
            P(("dp", "expert"), None, None),
            P(("dp", "expert"), None),
            P("expert", None, "dp"),
        ),
        check_vma=False,
    )
```

```python
import functools

import jax
import jax.numpy as jnp
from jax import lax
from jax.experimental import pallas as pl
from jax.experimental.pallas import tpu as pltpu
from jax.sharding import PartitionSpec as P

BF16 = jnp.bfloat16
F32 = jnp.float32


def slot_positions(routes_flat, experts, capacity):
    expert_ids = jnp.arange(experts, dtype=jnp.int32)
    onehot = (routes_flat[:, None] == expert_ids[None, :]).astype(BF16)
    ids = jnp.arange(routes_flat.shape[0], dtype=jnp.int32)
    before = (ids[None, :] < ids[:, None]).astype(BF16)
    counts = dot(before, onehot, ((1,), (0,)))
    rank = jnp.sum(counts * onehot.astype(F32), axis=1).astype(jnp.int32)
    return routes_flat * capacity + rank


def swiglu_parts(saved, hidden):
    gate_pre = saved[..., :hidden].astype(F32)
    up_pre = saved[..., hidden:].astype(F32)
    return (gate_pre, up_pre, jax.nn.silu(gate_pre))


def swiglu_grads(saved, weights, contraction, hidden):
    gate_pre, up_pre, active = swiglu_parts(saved, hidden)
    plain = (active * up_pre).astype(BF16)
    gate_grad = jnp.sum(plain.astype(F32) * contraction.astype(F32), axis=-1).astype(BF16)
    back = weights.astype(F32)[..., None] * contraction.astype(F32)
    sigma = jax.nn.sigmoid(gate_pre)
    grad_gate_pre = back * up_pre * sigma * (1.0 + gate_pre * (1.0 - sigma))
    grad_up_pre = back * active
    return (jnp.concatenate([grad_gate_pre, grad_up_pre], axis=-1).astype(BF16), gate_grad)


def scaled_hidden(saved, weights, hidden):
    gate_pre, up_pre, active = swiglu_parts(saved, hidden)
    return (weights.astype(F32)[..., None] * active * up_pre).astype(BF16)


def dot(a, b, dims):
    return lax.dot_general(a, b, (dims, ((), ())), preferred_element_type=F32)


def on_device_general(grad_out, saved_pre, gate_weight, routes, w_down):
    tokens_dev, top_count = routes.shape
    hidden = w_down.shape[1]
    half = w_down.shape[2]
    experts = lax.axis_size("expert")
    replicas = lax.axis_size("dp")
    capacity = 5 * tokens_dev * top_count // (4 * experts)
    slots = experts * capacity
    positions = slot_positions(routes.reshape(-1), experts, capacity).reshape(tokens_dev, top_count)
    slot_ids = jnp.arange(slots, dtype=jnp.int32)
    picks = [
        (positions[:, k][None, :] == slot_ids[:, None]).astype(BF16) for k in range(top_count)
    ]
    pick = sum(picks[1:], picks[0])
    devices = replicas * experts
    send_rows = jnp.stack(
        [
            dot(pick, grad_out[:, d * half : (d + 1) * half], ((1,), (0,))).astype(BF16)
            for d in range(replicas)
        ]
    ).reshape(devices, capacity, half)
    scaled = scaled_hidden(saved_pre, gate_weight, hidden)
    send_scaled = sum(dot(picks[k], scaled[:, k], ((1,), (0,))) for k in range(top_count))
    send_scaled = send_scaled.astype(BF16).reshape(experts, capacity, hidden)
    rows = lax.all_to_all(send_rows, ("dp", "expert"), split_axis=0, concat_axis=0, tiled=True)
    scaled_in = lax.all_to_all(send_scaled, "expert", split_axis=0, concat_axis=0, tiled=True)
    scaled_in = lax.all_gather(scaled_in.reshape(slots, hidden), "dp", axis=0, tiled=True)
    rows = rows.reshape(devices * capacity, half)
    partial = dot(rows, w_down[0], ((1,), (1,))).astype(BF16).reshape(devices, capacity, hidden)
    parts = lax.all_to_all(partial, ("dp", "expert"), split_axis=0, concat_axis=0, tiled=True)
    parts = parts.reshape(replicas, slots, hidden)
    contraction = jnp.stack(
        [
            sum(dot(picks[k], parts[d], ((0,), (0,))) for d in range(replicas))
            for k in range(top_count)
        ],
        axis=1,
    ).astype(BF16)
    grads, gate_grad = swiglu_grads(saved_pre, gate_weight, contraction, hidden)
    grad_down = dot(scaled_in, rows, ((0,), (0,))).astype(BF16)
    return grads, gate_grad, grad_down[None]


BASE = 16
MESH = pl.DeviceIdType.MESH


def iota(shape, axis):
    return lax.broadcasted_iota(jnp.int32, shape, axis)


def unfold_pick(groups, rest, q):
    shape = (groups * rest, groups * BASE)
    row, col = iota(shape, 0), iota(shape, 1)
    return (col == (row // rest) * BASE + q * rest + row % rest).astype(BF16)


def fold_pick(groups, rest, fold, q):
    shape = (groups * BASE, groups * rest)
    row, col = iota(shape, 0), iota(shape, 1)
    mine = (row // rest) % fold == q
    return (mine & (col == (row // BASE) * rest + row % rest)).astype(BF16)


def slot_keys(experts, rest, far, routes):
    tokens = routes.shape[1]
    names = iota((experts, tokens), 0)
    relative = [(routes[k : k + 1, :] + experts - far) % experts for k in range(2)]
    named = [(relative[k] == names).astype(F32) for k in range(2)]
    before = (iota((tokens, tokens), 0) < iota((tokens, tokens), 1)).astype(BF16)
    counts = dot((named[0] + named[1]).astype(BF16), before, ((1,), (0,)))
    keys = []
    for k in range(2):
        rank = jnp.sum(counts * named[k], axis=0, keepdims=True).astype(jnp.int32)
        keys.append(
            (
                jnp.where(rank < BASE, relative[k] * BASE + rank, -1),
                jnp.where(rank < BASE, -1, relative[k] * rest + rank - BASE),
            )
        )
    return keys


def exchange_kernel(
    experts, rest, fold, s_fold, chunks,
    routes_hbm, weights_hbm, rows_hbm, saved_hbm, w_hbm,
    pre_out, gate_out, down,
    routes, weights, rows, saved, w, pack, raw, names_in, relay_pick, relay, x_far, x, z,
    scaled, s_pack, s, s_wide, s_rest, s_turn, s_far, px_out, px_in, c_wide, c, r, c_routes, picks,
    grad_gate_factor, grad_up_factor, plain, key_col, left_col, weight_col, gate_col, total,
    load_sem, tn, rn, tw, rw, tm, rm, tg, rg, tss, rss, tf, rf, tp, rp, tb, rb,
):
    d = lax.axis_index("dp")
    e = lax.axis_index("expert")
    other = 1 - d
    me = d * experts + e
    half_experts = experts // 2
    at = e % half_experts
    near = (e // half_experts) * half_experts
    far = half_experts - near
    quarter = half_experts // 2
    lane, plane = at % quarter, at // quarter
    capacity = BASE + rest
    wide = 2 * capacity
    slab = relay_pick.shape[1] // half_experts
    gateway = quarter * (1 + far // half_experts) + lane
    is_gateway = (e // quarter) % 3 != 0
    tokens, width = rows.shape
    half = width // 2
    part = half // fold
    hidden = w.shape[0]
    part_s = hidden // s_fold
    group = half_experts * BASE
    rest_group = half_experts * rest
    count = experts * BASE

    def block(i):
        return pl.ds(pl.multiple_of(i * BASE, BASE), BASE)

    def remote(src, dst, send, recv, to):
        return pltpu.make_async_remote_copy(
            src_ref=src, dst_ref=dst, send_sem=send, recv_sem=recv, device_id=to, device_id_type=MESH
        )

    def wait_bytes(ref, sem):
        pltpu.make_async_copy(ref, ref, sem).wait()

    def loop(first, last, body):
        def step(k, carry):
            body(k)
            return carry

        lax.fori_loop(first, last, step, 0)

    loads = [
        pltpu.make_async_copy(source, target, load_sem.at[i])
        for i, (source, target) in enumerate(
            (
                (routes_hbm, routes), (rows_hbm, rows), (weights_hbm, weights), (saved_hbm, saved),
                (w_hbm, w),
            )
        )
    ]
    for load in loads:
        load.start()
    barrier = pltpu.get_barrier_semaphore()

    def greet(k):
        p = (me + k) % (2 * experts)
        pl.semaphore_signal(
            barrier, inc=1, device_id=(p // experts, p % experts), device_id_type=MESH
        )

    loop(1, 2 * experts, greet)

    loads[0].wait()
    (key0, left0), (key1, left1) = slot_keys(experts, rest, far, routes[...])
    row = iota((group, tokens), 0)
    main_pick = ((key0 == row + group) | (key1 == row + group)).astype(BF16)
    slot = (row // BASE) * rest + row % rest + rest_group
    hit = (left0 == slot) | (left1 == slot)
    left_pick = jnp.concatenate(
        [(hit & ((row // rest) % fold == q)).astype(BF16) for q in range(fold)], axis=1
    )

    def columns_of(h, lo, size):
        return pl.ds(pl.multiple_of(h * half + lo, 128), size)

    def pack_half(side, h):
        for lo in range(0, half, 512):
            pack[side, :, lo : lo + 512] = dot(
                main_pick, rows[:, columns_of(h, lo, 512)], ((1,), (0,))
            ).astype(BF16)
        folded = jnp.concatenate([rows[:, columns_of(h, q * part, part)] for q in range(fold)], axis=0)
        pack[side, :, half : half + part] = dot(left_pick, folded, ((1,), (0,))).astype(BF16)

    def near_copy(side, j):
        return remote(
            pack.at[side, block(j)],
            x.at[block(side * half_experts + at)],
            tn.at[side],
            rn.at[side],
            (other if side == 0 else d, near + j),
        )

    chunk, ahead, lead = half // chunks, 8, 5
    order = [(0, n) for n in range(lead)]
    for n in range(chunks):
        order += [(0, n + lead)] * (n + lead < chunks) + [(1, n)]

    def raw_copy(side, n):
        h = other if side == 0 else d
        return remote(
            rows.at[:, columns_of(h, n * chunk, chunk)],
            raw.at[side, pl.ds(pl.multiple_of(plane * tokens, tokens), tokens), n * chunk : (n + 1) * chunk],
            tw.at[side * chunks + n],
            rw.at[side * chunks + n],
            (h, gateway),
        )

    def names_copy(side):
        h = other if side == 0 else d
        return remote(routes, names_in.at[2 * side + plane], tm.at[0], rm.at[0], (h, gateway))

    loads[1].wait()
    pack_half(0, other)
    pack_half(1, d)
    pl.semaphore_wait(barrier, 2 * experts - 1)
    for side in range(2):
        names_copy(side).start()
    for side, n in order[:ahead]:
        raw_copy(side, n).start()

    def each_near(body):
        for k in range(quarter):
            for p in range(2):
                j = (plane if p == 0 else 1 - plane) * quarter + (lane + k) % quarter
                body(j, k == 0 and p == 0)

    def start_near_own(j, is_self):
        if not is_self:
            near_copy(1, j).start()

    def start_near_across(j, is_self):
        near_copy(0, j).start()

    each_near(start_near_own)
    pltpu.make_async_copy(
        pack.at[1, block(at)], x.at[block(half_experts + at)], rn.at[1]
    ).start()

    token_of = iota((2 * tokens, tokens), 0) // 2 == iota((2 * tokens, tokens), 1)
    first = iota((2 * tokens, tokens), 0) % 2 == 0

    def column(v0, v1):
        value = jnp.where(first, v0.astype(F32), v1.astype(F32))
        return jnp.sum(jnp.where(token_of, value, 0.0), axis=1, keepdims=True)

    loads[2].wait()
    key_col[...] = column(key0, key1).astype(jnp.int32)
    left_col[...] = column(left0, left1).astype(jnp.int32)
    weight_col[...] = column(weights[0:1, :], weights[1:2, :])
    loads[3].wait()
    step = 16

    @pl.loop(0, tokens // step)
    def _(i):
        mine = pl.ds(pl.multiple_of(i * 2 * step, 2 * step), 2 * step)
        both = saved[pl.ds(pl.multiple_of(i * step, step), step)].reshape(2 * step, 2 * hidden)
        gate_pre = both[:, :hidden].astype(F32)
        up_pre = both[:, hidden:].astype(F32)
        sigma = jax.nn.sigmoid(gate_pre)
        active = gate_pre * sigma
        weight = weight_col[mine, :]
        plain[mine, :] = (active * up_pre).astype(BF16)
        scaled[mine, :] = (weight * active * up_pre).astype(BF16)
        grad_up_factor[mine, :] = weight * active
        grad_gate_factor[mine, :] = weight * up_pre * sigma * (1.0 + gate_pre * (1.0 - sigma))

    slots = iota((2 * tokens, count), 1)

    picks[0] = (key_col[...] == slots).astype(BF16)
    wanted = (slots // BASE) * rest + slots % rest
    hit = left_col[...] == wanted
    for q in range(s_fold):
        picks[1 + q] = (hit & ((slots // rest) % fold == q)).astype(BF16)

    s_pack[:, 0:hidden] = dot(picks[0], scaled[...], ((0,), (0,))).astype(BF16)
    folded = jnp.zeros((count, part_s), F32)
    for q in range(s_fold):
        folded = folded + dot(
            picks[1 + q], scaled[:, q * part_s : (q + 1) * part_s], ((0,), (0,))
        )
    s_pack[:, hidden : hidden + part_s] = folded.astype(BF16)

    def scaled_copy(is_far, j):
        g = 1 if is_far else 3
        n = 1 + at if is_far else 0
        source = s_pack.at[block(j if is_far else half_experts + j)]
        to = (d, (far if is_far else near) + j)
        return remote(source, s.at[block(g * half_experts + at)], tss.at[int(is_far)], rss.at[n], to)

    def back_copy(is_far, j):
        n = 0 if is_far else 1
        source = c.at[block(j if is_far else half_experts + j)]
        to = (d, (far if is_far else near) + j)
        return remote(source, r.at[block(n * half_experts + at)], tb.at[n], rb.at[n], to)

    def rows_of(g):
        return slice(g * group, (g + 1) * group)

    def rest_of(g):
        return slice(g * rest_group, (g + 1) * rest_group)

    def slots_of(side):
        return slice(side * quarter * wide, (side + 1) * quarter * wide)

    def wide_pick(q, turned):
        shape = (quarter * wide, group) if turned else (group, quarter * wide)
        narrow, there = iota(shape, int(turned)), iota(shape, 1 - int(turned))
        source, inner = narrow // BASE, narrow % BASE
        base = (source % quarter) * wide + (source // quarter) * capacity
        if q is None:
            return (there == base + inner).astype(BF16)
        return ((there == base + BASE + inner % rest) & (inner // rest == q)).astype(BF16)

    def contract(n, side, put):
        if n == 0:
            lanes = slice(side * quarter, (side + 1) * quarter)
            wait_bytes(x_far.at[lanes], rg.at[side])
            lhs = x_far[lanes].reshape(quarter * wide, half)
        else:
            wait_bytes(x.at[rows_of(side)], rn.at[side])
            for q in range(fold):
                z[rest_of(side), q * part : (q + 1) * part] = dot(
                    unfold_pick(half_experts, rest, q),
                    x[rows_of(side), half : half + part],
                    ((1,), (0,)),
                ).astype(BF16)
            lhs = jnp.concatenate([x[rows_of(side), 0:half], z[rest_of(side), :]], axis=0)
        for lo in range(0, hidden, 256):
            put(lo, dot(lhs, w[lo : lo + 256, :], ((1,), (1,))))

    across = (other, e)

    def partial_copy(n):
        return remote(px_out.at[n], px_in.at[n], tp.at[n], rp.at[n], across)

    def forward_near():
        return remote(s.at[rows_of(3)], s.at[rows_of(2)], tf.at[0], rf.at[0], across)

    def forward_far(j):
        return remote(
            s.at[block(half_experts + j)], s.at[block(j)], tf.at[1 + j], rf.at[1 + j], across
        )

    loads[4].wait()

    def send_partial(n):
        def put(lo, value):
            px_out[n, :, lo : lo + 256] = value.astype(BF16)

        contract(n, 0, put)
        partial_copy(n).start()

    def finish(n):
        def put(lo, value):
            cut = slice(lo, lo + 256)
            summed = (value + px_in[n, :, cut].astype(F32)).astype(BF16)
            if n == 0:
                c_wide[:, cut] = summed
            else:
                c[rows_of(n), cut] = summed[:group]
                c_wide[0:rest_group, cut] = summed[group:]

        partial_copy(n).wait_recv()
        contract(n, 1, put)
        if n == 0:
            c[rows_of(n), 0:hidden] = dot(
                wide_pick(None, False), c_wide[...], ((1,), (0,))
            ).astype(BF16)
        folded = jnp.zeros((group, part_s), F32)
        for q in range(s_fold):
            cut = slice(q * part_s, (q + 1) * part_s)
            if n == 0:
                folded = folded + dot(wide_pick(q, False), c_wide[:, cut], ((1,), (0,)))
            else:
                folded = folded + dot(
                    fold_pick(half_experts, rest, fold, q), c_wide[0:rest_group, cut], ((1,), (0,))
                )
        c[rows_of(n), hidden : hidden + part_s] = folded.astype(BF16)

    def relay_copy(side, n, j):
        return remote(
            relay.at[side, n, j],
            x_far.at[side * quarter + lane, :, n * chunk : (n + 1) * chunk],
            tg.at[0],
            rg.at[side],
            (d, near + j),
        )

    def build_relay_pick():
        wait_bytes(names_in, rm.at[0])
        before = (iota((tokens, tokens), 0) < iota((tokens, tokens), 1)).astype(BF16)
        names = iota((half_experts, tokens), 0)
        target = iota((half_experts * slab, tokens), 0)
        for side in range(2):
            for p in range(2):
                named = [names_in[2 * side + p, k : k + 1, :] - near for k in range(2)]
                onehot = [(named[k] == names).astype(F32) for k in range(2)]
                counts = dot((onehot[0] + onehot[1]).astype(BF16), before, ((1,), (0,)))
                hits = []
                for k in range(2):
                    rank = jnp.sum(counts * onehot[k], axis=0, keepdims=True).astype(jnp.int32)
                    here = (named[k] >= 0) & (named[k] < half_experts)
                    hits.append(target == jnp.where(here, named[k] * slab + p * capacity + rank, -1))
                relay_pick[side, :, p * tokens : (p + 1) * tokens] = (hits[0] | hits[1]).astype(BF16)

    def relay_step(side, n):
        cut = slice(n * chunk, (n + 1) * chunk)
        wait_bytes(raw.at[side, :, cut], rw.at[side * chunks + n])
        packed = dot(relay_pick[side], raw[side, :, cut], ((1,), (0,))).astype(BF16)
        for j in range(half_experts):
            relay[side, n, j] = packed[j * slab : j * slab + wide]

        def start(j, is_self):
            if not is_self:
                relay_copy(side, n, j).start()

        each_near(start)
        pltpu.make_async_copy(
            relay.at[side, n, at],
            x_far.at[side * quarter + lane, :, cut],
            rg.at[side],
        ).start()

    def raw_steps(first, last):
        for i in range(first, last):

            @pl.when(is_gateway)
            def _():
                relay_step(*order[i])

            raw_copy(*order[i]).wait_send()
            if i + ahead < len(order):
                raw_copy(*order[i + ahead]).start()

    def scaled_start(is_far):
        def start(k):
            scaled_copy(is_far, (at + k) % half_experts).start()

        loop(0 if is_far else 1, half_experts, start)

    pl.when(is_gateway)(build_relay_pick)
    scaled_start(False)
    pltpu.make_async_copy(
        s_pack.at[block(half_experts + at)], s.at[block(3 * half_experts + at)], rss.at[0]
    ).start()
    raw_steps(0, 4)
    each_near(start_near_across)
    raw_steps(4, 8)
    wait_bytes(s.at[rows_of(3)], rss.at[0])
    forward_near().start()
    raw_steps(8, 14)
    send_partial(1)
    send_partial(0)
    raw_steps(14, 16)
    scaled_start(True)
    finish(0)
    def start_back_far(k):
        back_copy(True, (at + k) % half_experts).start()

    loop(0, half_experts, start_back_far)

    finish(1)
    def start_back_near(k):
        back_copy(False, (at + k) % half_experts).start()

    loop(1, half_experts, start_back_near)
    pltpu.make_async_copy(
        c.at[block(half_experts + at)], r.at[block(half_experts + at)], rb.at[1]
    ).start()


    def widen(side):
        for q in range(s_fold):
            cut = slice(q * part_s, (q + 1) * part_s)
            s_wide[slots_of(side), cut] = (
                dot(wide_pick(None, True), s[rows_of(side), cut], ((1,), (0,)))
                + dot(wide_pick(q, True), s[rows_of(side), hidden : hidden + part_s], ((1,), (0,)))
            ).astype(BF16)

    def turn_near():
        for side in range(2):
            for q in range(s_fold):
                s_rest[rest_of(side), q * part_s : (q + 1) * part_s] = dot(
                    unfold_pick(half_experts, rest, q),
                    s[rows_of(2 + side), hidden : hidden + part_s],
                    ((1,), (0,)),
                ).astype(BF16)
        s_turn[:, 0 : 2 * group] = s[2 * group : 4 * group, 0:hidden].T
        s_turn[:, 2 * group : 2 * group + 2 * rest_group] = s_rest[...].T

    def near_product(columns):
        return dot(s_turn[:, 0 : 2 * group], x[:, columns], ((1,), (0,))) + dot(
            s_turn[:, 2 * group : 2 * group + 2 * rest_group], z[:, columns], ((1,), (0,))
        )

    def far_product(side, columns):
        rhs = x_far[side * quarter : (side + 1) * quarter, :, columns]
        return dot(s_far[side], rhs.reshape(quarter * wide, columns.size), ((1,), (0,)))

    def each_columns(body):
        @pl.loop(0, half // 512)
        def _(j):
            body(pl.ds(pl.multiple_of(j * 512, 512), 512))

    forward_near().wait_recv()
    turn_near()

    def add_near(columns):
        total[:, columns] = near_product(columns)

    each_columns(add_near)

    def pass_on(k):
        j = (at + half_experts - k) % half_experts
        wait_bytes(s.at[block(half_experts + j)], rss.at[1 + j])
        forward_far(j).start()

    loop(0, half_experts, pass_on)
    widen(1)
    s_far[1] = s_wide[slots_of(1), :].T

    def add_own(columns):
        total[:, columns] = total[:, columns] + far_product(1, columns)

    each_columns(add_own)
    loop(0, half_experts, lambda j: forward_far(j).wait_recv())
    widen(0)
    s_far[0] = s_wide[slots_of(0), :].T

    def add_across(columns):
        down[:, columns] = (total[:, columns] + far_product(0, columns)).astype(BF16)

    each_columns(add_across)

    def unpermuted(n, q):
        cut = slice(q * part_s, (q + 1) * part_s)
        return dot(picks[0, :, rows_of(n)], r[rows_of(n), cut], ((1,), (0,))) + dot(
            picks[1 + q, :, rows_of(n)], r[rows_of(n), hidden : hidden + part_s], ((1,), (0,))
        )

    wait_bytes(r.at[rows_of(1)], rb.at[1])
    for q in range(s_fold):
        c_routes[:, q * part_s : (q + 1) * part_s] = unpermuted(1, q)
    wait_bytes(r.at[rows_of(0)], rb.at[0])
    for q in range(s_fold):
        cut = slice(q * part_s, (q + 1) * part_s)
        c_routes[:, cut] = c_routes[:, cut] + unpermuted(0, q)

    @pl.loop(0, tokens // step)
    def _(i):
        mine = pl.ds(pl.multiple_of(i * 2 * step, 2 * step), 2 * step)
        value = c_routes[mine, :]
        gate_col[mine, :] = jnp.sum(plain[mine, :].astype(F32) * value, axis=1, keepdims=True)
        out = jnp.concatenate(
            [value * grad_gate_factor[mine, :], value * grad_up_factor[mine, :]], axis=1
        ).astype(BF16)
        pre_out[pl.ds(pl.multiple_of(i * step, step), step)] = out.reshape(step, 2, 2 * hidden)

    for k in range(2):
        mine = token_of & (first if k == 0 else ~first)
        gate_out[k : k + 1, :] = jnp.sum(
            jnp.where(mine, gate_col[...], 0.0), axis=0, keepdims=True
        ).astype(BF16)

    wait_bytes(pack.at[0], tn.at[0])
    wait_bytes(pack.at[1, 0 : group - BASE], tn.at[1])
    wait_bytes(names_in.at[0:2], tm.at[0])

    @pl.when(is_gateway)
    def _():
        wait_bytes(relay.at[:, :, 0 : half_experts - 1], tg.at[0])

    wait_bytes(s_pack.at[0:group], tss.at[1])
    wait_bytes(s_pack.at[group : 2 * group - BASE], tss.at[0])
    wait_bytes(c.at[0:group], tb.at[0])
    wait_bytes(c.at[group : 2 * group - BASE], tb.at[1])
    for n in range(2):
        partial_copy(n).wait_send()
    forward_near().wait_send()
    loop(0, half_experts, lambda j: forward_far(j).wait_send())


def store_kernel(*refs):
    copies = [pltpu.make_async_copy(refs[i], refs[3 + i], refs[6].at[i]) for i in range(3)]
    for copy in copies:
        copy.start()
    for copy in copies:
        copy.wait()


def on_device(grad_out, saved_pre, gate_weight, routes, w_down):
    tokens, top_count = routes.shape
    hidden, half = w_down.shape[1:]
    width = grad_out.shape[1]
    experts = lax.axis_size("expert")
    replicas = lax.axis_size("dp")
    capacity = 5 * tokens * top_count // (4 * experts)
    if (replicas, top_count, experts, capacity, hidden, half % 512) != (2, 2, 16, 20, 768, 0):
        return on_device_general(grad_out, saved_pre, gate_weight, routes, w_down)
    rest = capacity - BASE
    fold = BASE // rest
    s_fold = hidden // 256
    devices = replicas * experts
    count, total = experts * BASE, devices * BASE
    part, part_s = half // fold, hidden // s_fold
    finished = (count + experts * rest) // 2
    chunks = half // 256
    vmem = pl.BlockSpec(memory_space=pltpu.VMEM)
    stored = pl.BlockSpec(memory_space=pltpu.HBM)
    dma = pltpu.SemaphoreType.DMA
    pre, gate, down = pl.pallas_call(
        functools.partial(exchange_kernel, experts, rest, fold, s_fold, chunks),
        out_shape=(
            pltpu.VMEM(saved_pre.shape, BF16),
            pltpu.VMEM((top_count, tokens), BF16),
            pltpu.VMEM((hidden, half), BF16),
        ),
        in_specs=[stored] * 5,
        out_specs=[vmem] * 3,
        scratch_shapes=[
            pltpu.VMEM((top_count, tokens), jnp.int32),
            pltpu.VMEM((top_count, tokens), BF16),
            pltpu.VMEM((tokens, width), BF16),
            pltpu.VMEM(saved_pre.shape, BF16),
            pltpu.VMEM((hidden, half), BF16),
            pltpu.VMEM((2, count // 2, half + part), BF16),
            pltpu.VMEM((2, 2 * tokens, half), BF16),
            pltpu.VMEM((4, top_count, tokens), jnp.int32),
            pltpu.VMEM((2, experts // 2 * -(-2 * capacity // 16) * 16, 2 * tokens), BF16),
            pltpu.VMEM((2, chunks, experts // 2, 2 * capacity, half // chunks), BF16),
            pltpu.VMEM((experts // 2, 2 * capacity, half), BF16),
            pltpu.VMEM((count, half + part), BF16),
            pltpu.VMEM((experts * rest, half), BF16),
            pltpu.VMEM((2 * tokens, hidden), BF16),
            pltpu.VMEM((count, hidden + part_s), BF16),
            pltpu.VMEM((total, hidden + part_s), BF16),
            pltpu.VMEM((2 * finished, hidden), BF16),
            pltpu.VMEM((experts * rest, hidden), BF16),
            pltpu.VMEM((hidden, 2 * finished), BF16),
            pltpu.VMEM((2, hidden, finished), BF16),
            pltpu.VMEM((2, finished, hidden), BF16),
            pltpu.VMEM((2, finished, hidden), BF16),
            pltpu.VMEM((finished, hidden), BF16),
            pltpu.VMEM((count, hidden + part_s), BF16),
            pltpu.VMEM((count, hidden + part_s), BF16),
            pltpu.VMEM((2 * tokens, hidden), F32),
            pltpu.VMEM((1 + s_fold, 2 * tokens, count), BF16),
            pltpu.VMEM((2 * tokens, hidden), F32),
            pltpu.VMEM((2 * tokens, hidden), F32),
            pltpu.VMEM((2 * tokens, hidden), BF16),
            pltpu.VMEM((2 * tokens, 1), jnp.int32),
            pltpu.VMEM((2 * tokens, 1), jnp.int32),
            pltpu.VMEM((2 * tokens, 1), F32),
            pltpu.VMEM((2 * tokens, 1), F32),
            pltpu.VMEM((hidden, half), F32),
            dma((5,)),
            dma((2,)), dma((2,)), dma((2 * chunks,)), dma((2 * chunks,)), dma((1,)), dma((1,)),
            dma((1,)), dma((2,)),
            dma((2,)), dma((experts,)), dma((experts,)), dma((experts,)),
            dma((2,)), dma((2,)), dma((2,)), dma((2,)),
        ],
        compiler_params=pltpu.CompilerParams(
            collective_id=0, has_side_effects=True, vmem_limit_bytes=40 << 20
        ),
    )(*[
        pltpu.with_memory_space_constraint(operand, pltpu.HBM)
        for operand in (routes.T, gate_weight.T, grad_out, saved_pre, w_down[0])
    ])
    pre, gate, down = pl.pallas_call(
        store_kernel,
        out_shape=[jax.ShapeDtypeStruct(a.shape, a.dtype) for a in (pre, gate, down)],
        in_specs=[vmem] * 3,
        out_specs=[stored] * 3,
        scratch_shapes=[dma((3,))],
        compiler_params=pltpu.CompilerParams(vmem_limit_bytes=1 << 20),
    )(pre, gate, down)
    return pre, gate.T, down[None]


def solution(mesh):
    return jax.shard_map(
        on_device,
        mesh=mesh,
        in_specs=(
            P(("dp", "expert"), None),
            P(("dp", "expert"), None, None),
            P(("dp", "expert"), None),
            P(("dp", "expert"), None),
            P("expert", None, "dp"),
        ),
        out_specs=(
            P(("dp", "expert"), None, None),
            P(("dp", "expert"), None),
            P("expert", None, "dp"),
        ),
        check_vma=False,
    )
```

```python
import functools

import jax
import jax.numpy as jnp
from jax import lax
from jax.experimental import pallas as pl
from jax.experimental.pallas import tpu as pltpu
from jax.sharding import PartitionSpec as P

BF16 = jnp.bfloat16
F32 = jnp.float32


def slot_positions(routes_flat, experts, capacity):
    expert_ids = jnp.arange(experts, dtype=jnp.int32)
    onehot = (routes_flat[:, None] == expert_ids[None, :]).astype(BF16)
    ids = jnp.arange(routes_flat.shape[0], dtype=jnp.int32)
    before = (ids[None, :] < ids[:, None]).astype(BF16)
    counts = dot(before, onehot, ((1,), (0,)))
    rank = jnp.sum(counts * onehot.astype(F32), axis=1).astype(jnp.int32)
    return routes_flat * capacity + rank


def swiglu_parts(saved, hidden):
    gate_pre = saved[..., :hidden].astype(F32)
    up_pre = saved[..., hidden:].astype(F32)
    return (gate_pre, up_pre, jax.nn.silu(gate_pre))


def swiglu_grads(saved, weights, contraction, hidden):
    gate_pre, up_pre, active = swiglu_parts(saved, hidden)
    plain = (active * up_pre).astype(BF16)
    gate_grad = jnp.sum(plain.astype(F32) * contraction.astype(F32), axis=-1).astype(BF16)
    back = weights.astype(F32)[..., None] * contraction.astype(F32)
    sigma = jax.nn.sigmoid(gate_pre)
    grad_gate_pre = back * up_pre * sigma * (1.0 + gate_pre * (1.0 - sigma))
    grad_up_pre = back * active
    return (jnp.concatenate([grad_gate_pre, grad_up_pre], axis=-1).astype(BF16), gate_grad)


def scaled_hidden(saved, weights, hidden):
    gate_pre, up_pre, active = swiglu_parts(saved, hidden)
    return (weights.astype(F32)[..., None] * active * up_pre).astype(BF16)


def dot(a, b, dims):
    return lax.dot_general(a, b, (dims, ((), ())), preferred_element_type=F32)


def on_device_general(grad_out, saved_pre, gate_weight, routes, w_down):
    tokens_dev, top_count = routes.shape
    hidden = w_down.shape[1]
    half = w_down.shape[2]
    experts = lax.axis_size("expert")
    replicas = lax.axis_size("dp")
    capacity = 5 * tokens_dev * top_count // (4 * experts)
    slots = experts * capacity
    positions = slot_positions(routes.reshape(-1), experts, capacity).reshape(tokens_dev, top_count)
    slot_ids = jnp.arange(slots, dtype=jnp.int32)
    picks = [
        (positions[:, k][None, :] == slot_ids[:, None]).astype(BF16) for k in range(top_count)
    ]
    pick = sum(picks[1:], picks[0])
    devices = replicas * experts
    send_rows = jnp.stack(
        [
            dot(pick, grad_out[:, d * half : (d + 1) * half], ((1,), (0,))).astype(BF16)
            for d in range(replicas)
        ]
    ).reshape(devices, capacity, half)
    scaled = scaled_hidden(saved_pre, gate_weight, hidden)
    send_scaled = sum(dot(picks[k], scaled[:, k], ((1,), (0,))) for k in range(top_count))
    send_scaled = send_scaled.astype(BF16).reshape(experts, capacity, hidden)
    rows = lax.all_to_all(send_rows, ("dp", "expert"), split_axis=0, concat_axis=0, tiled=True)
    scaled_in = lax.all_to_all(send_scaled, "expert", split_axis=0, concat_axis=0, tiled=True)
    scaled_in = lax.all_gather(scaled_in.reshape(slots, hidden), "dp", axis=0, tiled=True)
    rows = rows.reshape(devices * capacity, half)
    partial = dot(rows, w_down[0], ((1,), (1,))).astype(BF16).reshape(devices, capacity, hidden)
    parts = lax.all_to_all(partial, ("dp", "expert"), split_axis=0, concat_axis=0, tiled=True)
    parts = parts.reshape(replicas, slots, hidden)
    contraction = jnp.stack(
        [
            sum(dot(picks[k], parts[d], ((0,), (0,))) for d in range(replicas))
            for k in range(top_count)
        ],
        axis=1,
    ).astype(BF16)
    grads, gate_grad = swiglu_grads(saved_pre, gate_weight, contraction, hidden)
    grad_down = dot(scaled_in, rows, ((0,), (0,))).astype(BF16)
    return grads, gate_grad, grad_down[None]


BASE = 16
MESH = pl.DeviceIdType.MESH


def iota(shape, axis):
    return lax.broadcasted_iota(jnp.int32, shape, axis)


def unfold_pick(groups, rest, q):
    shape = (groups * rest, groups * BASE)
    row, col = iota(shape, 0), iota(shape, 1)
    return (col == (row // rest) * BASE + q * rest + row % rest).astype(BF16)


def fold_pick(groups, rest, fold, q):
    shape = (groups * BASE, groups * rest)
    row, col = iota(shape, 0), iota(shape, 1)
    mine = (row // rest) % fold == q
    return (mine & (col == (row // BASE) * rest + row % rest)).astype(BF16)


def slot_keys(experts, rest, far, routes):
    tokens = routes.shape[1]
    names = iota((experts, tokens), 0)
    relative = [(routes[k : k + 1, :] + experts - far) % experts for k in range(2)]
    named = [(relative[k] == names).astype(F32) for k in range(2)]
    before = (iota((tokens, tokens), 0) < iota((tokens, tokens), 1)).astype(BF16)
    counts = dot((named[0] + named[1]).astype(BF16), before, ((1,), (0,)))
    keys = []
    for k in range(2):
        rank = jnp.sum(counts * named[k], axis=0, keepdims=True).astype(jnp.int32)
        keys.append(
            (
                jnp.where(rank < BASE, relative[k] * BASE + rank, -1),
                jnp.where(rank < BASE, -1, relative[k] * rest + rank - BASE),
            )
        )
    return keys


def exchange_kernel(
    experts, rest, fold, s_fold, chunks,
    routes_hbm, weights_hbm, rows_hbm, saved_hbm, w_hbm,
    pre_out, gate_out, down,
    routes, weights, rows, saved, w, pack, raw, names_in, relay_pick, relay, x_far, x, z,
    scaled, s_pack, s, s_wide, s_rest, s_turn, s_far, px_out, px_in, c_wide, c, r, c_routes, picks,
    grad_gate_factor, grad_up_factor, plain, key_col, left_col, weight_col, gate_col, total,
    load_sem, tn, rn, tw, rw, tm, rm, tg, rg, tss, rss, tf, rf, tp, rp, tb, rb,
):
    d = lax.axis_index("dp")
    e = lax.axis_index("expert")
    other = 1 - d
    me = d * experts + e
    half_experts = experts // 2
    at = e % half_experts
    near = (e // half_experts) * half_experts
    far = half_experts - near
    quarter = half_experts // 2
    lane, plane = at % quarter, at // quarter
    capacity = BASE + rest
    wide = 2 * capacity
    slab = relay_pick.shape[1] // half_experts
    gateway = quarter * (1 + far // half_experts) + lane
    is_gateway = (e // quarter) % 3 != 0
    tokens, width = rows.shape
    half = width // 2
    part = half // fold
    hidden = w.shape[0]
    part_s = hidden // s_fold
    group = half_experts * BASE
    rest_group = half_experts * rest
    count = experts * BASE

    def block(i):
        return pl.ds(pl.multiple_of(i * BASE, BASE), BASE)

    def remote(src, dst, send, recv, to):
        return pltpu.make_async_remote_copy(
            src_ref=src, dst_ref=dst, send_sem=send, recv_sem=recv, device_id=to, device_id_type=MESH
        )

    def wait_bytes(ref, sem):
        pltpu.make_async_copy(ref, ref, sem).wait()

    def loop(first, last, body):
        def step(k, carry):
            body(k)
            return carry

        lax.fori_loop(first, last, step, 0)

    loads = [
        pltpu.make_async_copy(source, target, load_sem.at[i])
        for i, (source, target) in enumerate(
            (
                (routes_hbm, routes), (rows_hbm, rows), (weights_hbm, weights), (saved_hbm, saved),
                (w_hbm, w),
            )
        )
    ]
    for load in loads:
        load.start()
    barrier = pltpu.get_barrier_semaphore()

    def greet(k):
        p = (me + k) % (2 * experts)
        pl.semaphore_signal(
            barrier, inc=1, device_id=(p // experts, p % experts), device_id_type=MESH
        )

    loop(1, 2 * experts, greet)

    loads[0].wait()
    (key0, left0), (key1, left1) = slot_keys(experts, rest, far, routes[...])
    row = iota((group, tokens), 0)
    main_pick = ((key0 == row + group) | (key1 == row + group)).astype(BF16)
    slot = (row // BASE) * rest + row % rest + rest_group
    hit = (left0 == slot) | (left1 == slot)
    left_pick = jnp.concatenate(
        [(hit & ((row // rest) % fold == q)).astype(BF16) for q in range(fold)], axis=1
    )

    def columns_of(h, lo, size):
        return pl.ds(pl.multiple_of(h * half + lo, 128), size)

    def pack_half(side, h):
        for lo in range(0, half, 512):
            pack[side, :, lo : lo + 512] = dot(
                main_pick, rows[:, columns_of(h, lo, 512)], ((1,), (0,))
            ).astype(BF16)
        folded = jnp.concatenate([rows[:, columns_of(h, q * part, part)] for q in range(fold)], axis=0)
        pack[side, :, half : half + part] = dot(left_pick, folded, ((1,), (0,))).astype(BF16)

    def near_copy(side, j):
        return remote(
            pack.at[side, block(j)],
            x.at[block(side * half_experts + at)],
            tn.at[side],
            rn.at[side],
            (other if side == 0 else d, near + j),
        )

    chunk, ahead, lead = half // chunks, 8, 6
    order = [(0, n) for n in range(lead)]
    for n in range(chunks):
        order += [(0, n + lead)] * (n + lead < chunks) + [(1, n)]

    def raw_copy(side, n):
        h = other if side == 0 else d
        return remote(
            rows.at[:, columns_of(h, n * chunk, chunk)],
            raw.at[side, pl.ds(pl.multiple_of(plane * tokens, tokens), tokens), n * chunk : (n + 1) * chunk],
            tw.at[side * chunks + n],
            rw.at[side * chunks + n],
            (h, gateway),
        )

    def names_copy(side):
        h = other if side == 0 else d
        return remote(routes, names_in.at[2 * side + plane], tm.at[0], rm.at[0], (h, gateway))

    loads[1].wait()
    pack_half(0, other)
    pack_half(1, d)
    pl.semaphore_wait(barrier, 2 * experts - 1)
    for side in range(2):
        names_copy(side).start()
    for side, n in order[:ahead]:
        raw_copy(side, n).start()

    def each_near(body):
        for k in range(quarter):
            for p in range(2):
                j = (plane if p == 0 else 1 - plane) * quarter + (lane + k) % quarter
                body(j, k == 0 and p == 0)

    def start_near_own(j, is_self):
        if not is_self:
            near_copy(1, j).start()

    def start_near_across(j, is_self):
        near_copy(0, j).start()

    each_near(start_near_own)
    pltpu.make_async_copy(
        pack.at[1, block(at)], x.at[block(half_experts + at)], rn.at[1]
    ).start()

    token_of = iota((2 * tokens, tokens), 0) // 2 == iota((2 * tokens, tokens), 1)
    first = iota((2 * tokens, tokens), 0) % 2 == 0

    def column(v0, v1):
        value = jnp.where(first, v0.astype(F32), v1.astype(F32))
        return jnp.sum(jnp.where(token_of, value, 0.0), axis=1, keepdims=True)

    loads[2].wait()
    key_col[...] = column(key0, key1).astype(jnp.int32)
    left_col[...] = column(left0, left1).astype(jnp.int32)
    weight_col[...] = column(weights[0:1, :], weights[1:2, :])
    loads[3].wait()
    step = 16

    @pl.loop(0, tokens // step)
    def _(i):
        mine = pl.ds(pl.multiple_of(i * 2 * step, 2 * step), 2 * step)
        both = saved[pl.ds(pl.multiple_of(i * step, step), step)].reshape(2 * step, 2 * hidden)
        gate_pre = both[:, :hidden].astype(F32)
        up_pre = both[:, hidden:].astype(F32)
        sigma = jax.nn.sigmoid(gate_pre)
        active = gate_pre * sigma
        weight = weight_col[mine, :]
        plain[mine, :] = (active * up_pre).astype(BF16)
        scaled[mine, :] = (weight * active * up_pre).astype(BF16)
        grad_up_factor[mine, :] = weight * active
        grad_gate_factor[mine, :] = weight * up_pre * sigma * (1.0 + gate_pre * (1.0 - sigma))

    slots = iota((2 * tokens, count), 1)

    picks[0] = (key_col[...] == slots).astype(BF16)
    wanted = (slots // BASE) * rest + slots % rest
    hit = left_col[...] == wanted
    for q in range(s_fold):
        picks[1 + q] = (hit & ((slots // rest) % fold == q)).astype(BF16)

    s_pack[:, 0:hidden] = dot(picks[0], scaled[...], ((0,), (0,))).astype(BF16)
    folded = jnp.zeros((count, part_s), F32)
    for q in range(s_fold):
        folded = folded + dot(
            picks[1 + q], scaled[:, q * part_s : (q + 1) * part_s], ((0,), (0,))
        )
    s_pack[:, hidden : hidden + part_s] = folded.astype(BF16)

    def scaled_copy(is_far, j):
        g = 1 if is_far else 3
        n = 1 + at if is_far else 0
        source = s_pack.at[block(j if is_far else half_experts + j)]
        to = (d, (far if is_far else near) + j)
        return remote(source, s.at[block(g * half_experts + at)], tss.at[int(is_far)], rss.at[n], to)

    def back_copy(is_far, j):
        n = 0 if is_far else 1
        source = c.at[block(j if is_far else half_experts + j)]
        to = (d, (far if is_far else near) + j)
        return remote(source, r.at[block(n * half_experts + at)], tb.at[n], rb.at[n], to)

    def rows_of(g):
        return slice(g * group, (g + 1) * group)

    def rest_of(g):
        return slice(g * rest_group, (g + 1) * rest_group)

    def slots_of(side):
        return slice(side * quarter * wide, (side + 1) * quarter * wide)

    def wide_pick(q, turned):
        shape = (quarter * wide, group) if turned else (group, quarter * wide)
        narrow, there = iota(shape, int(turned)), iota(shape, 1 - int(turned))
        source, inner = narrow // BASE, narrow % BASE
        base = (source % quarter) * wide + (source // quarter) * capacity
        if q is None:
            return (there == base + inner).astype(BF16)
        return ((there == base + BASE + inner % rest) & (inner // rest == q)).astype(BF16)

    def contract(n, side, put):
        if n == 0:
            lanes = slice(side * quarter, (side + 1) * quarter)
            wait_bytes(x_far.at[lanes], rg.at[side])
            lhs = x_far[lanes].reshape(quarter * wide, half)
        else:
            wait_bytes(x.at[rows_of(side)], rn.at[side])
            for q in range(fold):
                z[rest_of(side), q * part : (q + 1) * part] = dot(
                    unfold_pick(half_experts, rest, q),
                    x[rows_of(side), half : half + part],
                    ((1,), (0,)),
                ).astype(BF16)
            lhs = jnp.concatenate([x[rows_of(side), 0:half], z[rest_of(side), :]], axis=0)
        for lo in range(0, hidden, 256):
            put(lo, dot(lhs, w[lo : lo + 256, :], ((1,), (1,))))

    across = (other, e)

    def partial_copy(n):
        return remote(px_out.at[n], px_in.at[n], tp.at[n], rp.at[n], across)

    def forward_near():
        return remote(s.at[rows_of(3)], s.at[rows_of(2)], tf.at[0], rf.at[0], across)

    def forward_far(j):
        return remote(
            s.at[block(half_experts + j)], s.at[block(j)], tf.at[1 + j], rf.at[1 + j], across
        )

    loads[4].wait()

    def send_partial(n):
        def put(lo, value):
            px_out[n, :, lo : lo + 256] = value.astype(BF16)

        contract(n, 0, put)
        partial_copy(n).start()

    def finish(n):
        def put(lo, value):
            cut = slice(lo, lo + 256)
            summed = (value + px_in[n, :, cut].astype(F32)).astype(BF16)
            if n == 0:
                c_wide[:, cut] = summed
            else:
                c[rows_of(n), cut] = summed[:group]
                c_wide[0:rest_group, cut] = summed[group:]

        partial_copy(n).wait_recv()
        contract(n, 1, put)
        if n == 0:
            c[rows_of(n), 0:hidden] = dot(
                wide_pick(None, False), c_wide[...], ((1,), (0,))
            ).astype(BF16)
        folded = jnp.zeros((group, part_s), F32)
        for q in range(s_fold):
            cut = slice(q * part_s, (q + 1) * part_s)
            if n == 0:
                folded = folded + dot(wide_pick(q, False), c_wide[:, cut], ((1,), (0,)))
            else:
                folded = folded + dot(
                    fold_pick(half_experts, rest, fold, q), c_wide[0:rest_group, cut], ((1,), (0,))
                )
        c[rows_of(n), hidden : hidden + part_s] = folded.astype(BF16)

    def relay_copy(side, n, j):
        return remote(
            relay.at[side, n, j],
            x_far.at[side * quarter + lane, :, n * chunk : (n + 1) * chunk],
            tg.at[0],
            rg.at[side],
            (d, near + j),
        )

    def build_relay_pick():
        wait_bytes(names_in, rm.at[0])
        before = (iota((tokens, tokens), 0) < iota((tokens, tokens), 1)).astype(BF16)
        names = iota((half_experts, tokens), 0)
        target = iota((half_experts * slab, tokens), 0)
        for side in range(2):
            for p in range(2):
                named = [names_in[2 * side + p, k : k + 1, :] - near for k in range(2)]
                onehot = [(named[k] == names).astype(F32) for k in range(2)]
                counts = dot((onehot[0] + onehot[1]).astype(BF16), before, ((1,), (0,)))
                hits = []
                for k in range(2):
                    rank = jnp.sum(counts * onehot[k], axis=0, keepdims=True).astype(jnp.int32)
                    here = (named[k] >= 0) & (named[k] < half_experts)
                    hits.append(target == jnp.where(here, named[k] * slab + p * capacity + rank, -1))
                relay_pick[side, :, p * tokens : (p + 1) * tokens] = (hits[0] | hits[1]).astype(BF16)

    def relay_step(side, n):
        cut = slice(n * chunk, (n + 1) * chunk)
        wait_bytes(raw.at[side, :, cut], rw.at[side * chunks + n])
        packed = dot(relay_pick[side], raw[side, :, cut], ((1,), (0,))).astype(BF16)
        for j in range(half_experts):
            relay[side, n, j] = packed[j * slab : j * slab + wide]

        def start(j, is_self):
            if not is_self:
                relay_copy(side, n, j).start()

        each_near(start)
        pltpu.make_async_copy(
            relay.at[side, n, at],
            x_far.at[side * quarter + lane, :, cut],
            rg.at[side],
        ).start()

    def raw_steps(first, last):
        for i in range(first, last):

            @pl.when(is_gateway)
            def _():
                relay_step(*order[i])

            raw_copy(*order[i]).wait_send()
            if i + ahead < len(order):
                raw_copy(*order[i + ahead]).start()

    def scaled_start(is_far):
        def start(k):
            scaled_copy(is_far, (at + k) % half_experts).start()

        loop(0 if is_far else 1, half_experts, start)

    pl.when(is_gateway)(build_relay_pick)
    scaled_start(False)
    pltpu.make_async_copy(
        s_pack.at[block(half_experts + at)], s.at[block(3 * half_experts + at)], rss.at[0]
    ).start()
    raw_steps(0, 6)
    each_near(start_near_across)
    raw_steps(6, 8)
    wait_bytes(s.at[rows_of(3)], rss.at[0])
    forward_near().start()
    raw_steps(8, 14)
    send_partial(0)
    raw_steps(14, 16)
    send_partial(1)
    scaled_start(True)
    finish(0)
    def start_back_far(k):
        back_copy(True, (at + k) % half_experts).start()

    loop(0, half_experts, start_back_far)

    finish(1)
    def start_back_near(k):
        back_copy(False, (at + k) % half_experts).start()

    loop(1, half_experts, start_back_near)
    pltpu.make_async_copy(
        c.at[block(half_experts + at)], r.at[block(half_experts + at)], rb.at[1]
    ).start()


    def widen(side):
        for q in range(s_fold):
            cut = slice(q * part_s, (q + 1) * part_s)
            s_wide[slots_of(side), cut] = (
                dot(wide_pick(None, True), s[rows_of(side), cut], ((1,), (0,)))
                + dot(wide_pick(q, True), s[rows_of(side), hidden : hidden + part_s], ((1,), (0,)))
            ).astype(BF16)

    def turn_near():
        for side in range(2):
            for q in range(s_fold):
                s_rest[rest_of(side), q * part_s : (q + 1) * part_s] = dot(
                    unfold_pick(half_experts, rest, q),
                    s[rows_of(2 + side), hidden : hidden + part_s],
                    ((1,), (0,)),
                ).astype(BF16)
        s_turn[:, 0 : 2 * group] = s[2 * group : 4 * group, 0:hidden].T
        s_turn[:, 2 * group : 2 * group + 2 * rest_group] = s_rest[...].T

    def near_product(columns):
        return dot(s_turn[:, 0 : 2 * group], x[:, columns], ((1,), (0,))) + dot(
            s_turn[:, 2 * group : 2 * group + 2 * rest_group], z[:, columns], ((1,), (0,))
        )

    def far_product(side, columns):
        rhs = x_far[side * quarter : (side + 1) * quarter, :, columns]
        return dot(s_far[side], rhs.reshape(quarter * wide, columns.size), ((1,), (0,)))

    def each_columns(body):
        @pl.loop(0, half // 512)
        def _(j):
            body(pl.ds(pl.multiple_of(j * 512, 512), 512))

    forward_near().wait_recv()
    turn_near()

    def add_near(columns):
        total[:, columns] = near_product(columns)

    each_columns(add_near)

    def pass_on(k):
        j = (at + half_experts - k) % half_experts
        wait_bytes(s.at[block(half_experts + j)], rss.at[1 + j])
        forward_far(j).start()

    loop(0, half_experts, pass_on)
    widen(1)
    s_far[1] = s_wide[slots_of(1), :].T

    def add_own(columns):
        total[:, columns] = total[:, columns] + far_product(1, columns)

    each_columns(add_own)
    loop(0, half_experts, lambda j: forward_far(j).wait_recv())
    widen(0)
    s_far[0] = s_wide[slots_of(0), :].T

    def add_across(columns):
        down[:, columns] = (total[:, columns] + far_product(0, columns)).astype(BF16)

    each_columns(add_across)

    def unpermuted(n, q):
        cut = slice(q * part_s, (q + 1) * part_s)
        return dot(picks[0, :, rows_of(n)], r[rows_of(n), cut], ((1,), (0,))) + dot(
            picks[1 + q, :, rows_of(n)], r[rows_of(n), hidden : hidden + part_s], ((1,), (0,))
        )

    wait_bytes(r.at[rows_of(1)], rb.at[1])
    for q in range(s_fold):
        c_routes[:, q * part_s : (q + 1) * part_s] = unpermuted(1, q)
    wait_bytes(r.at[rows_of(0)], rb.at[0])
    for q in range(s_fold):
        cut = slice(q * part_s, (q + 1) * part_s)
        c_routes[:, cut] = c_routes[:, cut] + unpermuted(0, q)

    @pl.loop(0, tokens // step)
    def _(i):
        mine = pl.ds(pl.multiple_of(i * 2 * step, 2 * step), 2 * step)
        value = c_routes[mine, :]
        gate_col[mine, :] = jnp.sum(plain[mine, :].astype(F32) * value, axis=1, keepdims=True)
        out = jnp.concatenate(
            [value * grad_gate_factor[mine, :], value * grad_up_factor[mine, :]], axis=1
        ).astype(BF16)
        pre_out[pl.ds(pl.multiple_of(i * step, step), step)] = out.reshape(step, 2, 2 * hidden)

    for k in range(2):
        mine = token_of & (first if k == 0 else ~first)
        gate_out[k : k + 1, :] = jnp.sum(
            jnp.where(mine, gate_col[...], 0.0), axis=0, keepdims=True
        ).astype(BF16)

    wait_bytes(pack.at[0], tn.at[0])
    wait_bytes(pack.at[1, 0 : group - BASE], tn.at[1])
    wait_bytes(names_in.at[0:2], tm.at[0])

    @pl.when(is_gateway)
    def _():
        wait_bytes(relay.at[:, :, 0 : half_experts - 1], tg.at[0])

    wait_bytes(s_pack.at[0:group], tss.at[1])
    wait_bytes(s_pack.at[group : 2 * group - BASE], tss.at[0])
    wait_bytes(c.at[0:group], tb.at[0])
    wait_bytes(c.at[group : 2 * group - BASE], tb.at[1])
    for n in range(2):
        partial_copy(n).wait_send()
    forward_near().wait_send()
    loop(0, half_experts, lambda j: forward_far(j).wait_send())


def store_kernel(*refs):
    copies = [pltpu.make_async_copy(refs[i], refs[3 + i], refs[6].at[i]) for i in range(3)]
    for copy in copies:
        copy.start()
    for copy in copies:
        copy.wait()


def on_device(grad_out, saved_pre, gate_weight, routes, w_down):
    tokens, top_count = routes.shape
    hidden, half = w_down.shape[1:]
    width = grad_out.shape[1]
    experts = lax.axis_size("expert")
    replicas = lax.axis_size("dp")
    capacity = 5 * tokens * top_count // (4 * experts)
    if (replicas, top_count, experts, capacity, hidden, half % 512) != (2, 2, 16, 20, 768, 0):
        return on_device_general(grad_out, saved_pre, gate_weight, routes, w_down)
    rest = capacity - BASE
    fold = BASE // rest
    s_fold = hidden // 256
    devices = replicas * experts
    count, total = experts * BASE, devices * BASE
    part, part_s = half // fold, hidden // s_fold
    finished = (count + experts * rest) // 2
    chunks = half // 256
    vmem = pl.BlockSpec(memory_space=pltpu.VMEM)
    stored = pl.BlockSpec(memory_space=pltpu.HBM)
    dma = pltpu.SemaphoreType.DMA
    pre, gate, down = pl.pallas_call(
        functools.partial(exchange_kernel, experts, rest, fold, s_fold, chunks),
        out_shape=(
            pltpu.VMEM(saved_pre.shape, BF16),
            pltpu.VMEM((top_count, tokens), BF16),
            pltpu.VMEM((hidden, half), BF16),
        ),
        in_specs=[stored] * 5,
        out_specs=[vmem] * 3,
        scratch_shapes=[
            pltpu.VMEM((top_count, tokens), jnp.int32),
            pltpu.VMEM((top_count, tokens), BF16),
            pltpu.VMEM((tokens, width), BF16),
            pltpu.VMEM(saved_pre.shape, BF16),
            pltpu.VMEM((hidden, half), BF16),
            pltpu.VMEM((2, count // 2, half + part), BF16),
            pltpu.VMEM((2, 2 * tokens, half), BF16),
            pltpu.VMEM((4, top_count, tokens), jnp.int32),
            pltpu.VMEM((2, experts // 2 * -(-2 * capacity // 16) * 16, 2 * tokens), BF16),
            pltpu.VMEM((2, chunks, experts // 2, 2 * capacity, half // chunks), BF16),
            pltpu.VMEM((experts // 2, 2 * capacity, half), BF16),
            pltpu.VMEM((count, half + part), BF16),
            pltpu.VMEM((experts * rest, half), BF16),
            pltpu.VMEM((2 * tokens, hidden), BF16),
            pltpu.VMEM((count, hidden + part_s), BF16),
            pltpu.VMEM((total, hidden + part_s), BF16),
            pltpu.VMEM((2 * finished, hidden), BF16),
            pltpu.VMEM((experts * rest, hidden), BF16),
            pltpu.VMEM((hidden, 2 * finished), BF16),
            pltpu.VMEM((2, hidden, finished), BF16),
            pltpu.VMEM((2, finished, hidden), BF16),
            pltpu.VMEM((2, finished, hidden), BF16),
            pltpu.VMEM((finished, hidden), BF16),
            pltpu.VMEM((count, hidden + part_s), BF16),
            pltpu.VMEM((count, hidden + part_s), BF16),
            pltpu.VMEM((2 * tokens, hidden), F32),
            pltpu.VMEM((1 + s_fold, 2 * tokens, count), BF16),
            pltpu.VMEM((2 * tokens, hidden), F32),
            pltpu.VMEM((2 * tokens, hidden), F32),
            pltpu.VMEM((2 * tokens, hidden), BF16),
            pltpu.VMEM((2 * tokens, 1), jnp.int32),
            pltpu.VMEM((2 * tokens, 1), jnp.int32),
            pltpu.VMEM((2 * tokens, 1), F32),
            pltpu.VMEM((2 * tokens, 1), F32),
            pltpu.VMEM((hidden, half), F32),
            dma((5,)),
            dma((2,)), dma((2,)), dma((2 * chunks,)), dma((2 * chunks,)), dma((1,)), dma((1,)),
            dma((1,)), dma((2,)),
            dma((2,)), dma((experts,)), dma((experts,)), dma((experts,)),
            dma((2,)), dma((2,)), dma((2,)), dma((2,)),
        ],
        compiler_params=pltpu.CompilerParams(
            collective_id=0, has_side_effects=True, vmem_limit_bytes=40 << 20
        ),
    )(*[
        pltpu.with_memory_space_constraint(operand, pltpu.HBM)
        for operand in (routes.T, gate_weight.T, grad_out, saved_pre, w_down[0])
    ])
    pre, gate, down = pl.pallas_call(
        store_kernel,
        out_shape=[jax.ShapeDtypeStruct(a.shape, a.dtype) for a in (pre, gate, down)],
        in_specs=[vmem] * 3,
        out_specs=[stored] * 3,
        scratch_shapes=[dma((3,))],
        compiler_params=pltpu.CompilerParams(vmem_limit_bytes=1 << 20),
    )(pre, gate, down)
    return pre, gate.T, down[None]


def solution(mesh):
    return jax.shard_map(
        on_device,
        mesh=mesh,
        in_specs=(
            P(("dp", "expert"), None),
            P(("dp", "expert"), None, None),
            P(("dp", "expert"), None),
            P(("dp", "expert"), None),
            P("expert", None, "dp"),
        ),
        out_specs=(
            P(("dp", "expert"), None, None),
            P(("dp", "expert"), None),
            P("expert", None, "dp"),
        ),
        check_vma=False,
    )
```

```python
import functools

import jax
import jax.numpy as jnp
from jax import lax
from jax.experimental import pallas as pl
from jax.experimental.pallas import tpu as pltpu
from jax.sharding import PartitionSpec as P

BF16 = jnp.bfloat16
F32 = jnp.float32


def slot_positions(routes_flat, experts, capacity):
    expert_ids = jnp.arange(experts, dtype=jnp.int32)
    onehot = (routes_flat[:, None] == expert_ids[None, :]).astype(BF16)
    ids = jnp.arange(routes_flat.shape[0], dtype=jnp.int32)
    before = (ids[None, :] < ids[:, None]).astype(BF16)
    counts = dot(before, onehot, ((1,), (0,)))
    rank = jnp.sum(counts * onehot.astype(F32), axis=1).astype(jnp.int32)
    return routes_flat * capacity + rank


def swiglu_parts(saved, hidden):
    gate_pre = saved[..., :hidden].astype(F32)
    up_pre = saved[..., hidden:].astype(F32)
    return (gate_pre, up_pre, jax.nn.silu(gate_pre))


def swiglu_grads(saved, weights, contraction, hidden):
    gate_pre, up_pre, active = swiglu_parts(saved, hidden)
    plain = (active * up_pre).astype(BF16)
    gate_grad = jnp.sum(plain.astype(F32) * contraction.astype(F32), axis=-1).astype(BF16)
    back = weights.astype(F32)[..., None] * contraction.astype(F32)
    sigma = jax.nn.sigmoid(gate_pre)
    grad_gate_pre = back * up_pre * sigma * (1.0 + gate_pre * (1.0 - sigma))
    grad_up_pre = back * active
    return (jnp.concatenate([grad_gate_pre, grad_up_pre], axis=-1).astype(BF16), gate_grad)


def scaled_hidden(saved, weights, hidden):
    gate_pre, up_pre, active = swiglu_parts(saved, hidden)
    return (weights.astype(F32)[..., None] * active * up_pre).astype(BF16)


def dot(a, b, dims):
    return lax.dot_general(a, b, (dims, ((), ())), preferred_element_type=F32)


def on_device_general(grad_out, saved_pre, gate_weight, routes, w_down):
    tokens_dev, top_count = routes.shape
    hidden = w_down.shape[1]
    half = w_down.shape[2]
    experts = lax.axis_size("expert")
    replicas = lax.axis_size("dp")
    capacity = 5 * tokens_dev * top_count // (4 * experts)
    slots = experts * capacity
    positions = slot_positions(routes.reshape(-1), experts, capacity).reshape(tokens_dev, top_count)
    slot_ids = jnp.arange(slots, dtype=jnp.int32)
    picks = [
        (positions[:, k][None, :] == slot_ids[:, None]).astype(BF16) for k in range(top_count)
    ]
    pick = sum(picks[1:], picks[0])
    devices = replicas * experts
    send_rows = jnp.stack(
        [
            dot(pick, grad_out[:, d * half : (d + 1) * half], ((1,), (0,))).astype(BF16)
            for d in range(replicas)
        ]
    ).reshape(devices, capacity, half)
    scaled = scaled_hidden(saved_pre, gate_weight, hidden)
    send_scaled = sum(dot(picks[k], scaled[:, k], ((1,), (0,))) for k in range(top_count))
    send_scaled = send_scaled.astype(BF16).reshape(experts, capacity, hidden)
    rows = lax.all_to_all(send_rows, ("dp", "expert"), split_axis=0, concat_axis=0, tiled=True)
    scaled_in = lax.all_to_all(send_scaled, "expert", split_axis=0, concat_axis=0, tiled=True)
    scaled_in = lax.all_gather(scaled_in.reshape(slots, hidden), "dp", axis=0, tiled=True)
    rows = rows.reshape(devices * capacity, half)
    partial = dot(rows, w_down[0], ((1,), (1,))).astype(BF16).reshape(devices, capacity, hidden)
    parts = lax.all_to_all(partial, ("dp", "expert"), split_axis=0, concat_axis=0, tiled=True)
    parts = parts.reshape(replicas, slots, hidden)
    contraction = jnp.stack(
        [
            sum(dot(picks[k], parts[d], ((0,), (0,))) for d in range(replicas))
            for k in range(top_count)
        ],
        axis=1,
    ).astype(BF16)
    grads, gate_grad = swiglu_grads(saved_pre, gate_weight, contraction, hidden)
    grad_down = dot(scaled_in, rows, ((0,), (0,))).astype(BF16)
    return grads, gate_grad, grad_down[None]


BASE = 16
MESH = pl.DeviceIdType.MESH


def iota(shape, axis):
    return lax.broadcasted_iota(jnp.int32, shape, axis)


def unfold_pick(groups, rest, q):
    shape = (groups * rest, groups * BASE)
    row, col = iota(shape, 0), iota(shape, 1)
    return (col == (row // rest) * BASE + q * rest + row % rest).astype(BF16)


def fold_pick(groups, rest, fold, q):
    shape = (groups * BASE, groups * rest)
    row, col = iota(shape, 0), iota(shape, 1)
    mine = (row // rest) % fold == q
    return (mine & (col == (row // BASE) * rest + row % rest)).astype(BF16)


def slot_keys(experts, rest, far, routes):
    tokens = routes.shape[1]
    names = iota((experts, tokens), 0)
    relative = [(routes[k : k + 1, :] + experts - far) % experts for k in range(2)]
    named = [(relative[k] == names).astype(F32) for k in range(2)]
    before = (iota((tokens, tokens), 0) < iota((tokens, tokens), 1)).astype(BF16)
    counts = dot((named[0] + named[1]).astype(BF16), before, ((1,), (0,)))
    keys = []
    for k in range(2):
        rank = jnp.sum(counts * named[k], axis=0, keepdims=True).astype(jnp.int32)
        keys.append(
            (
                jnp.where(rank < BASE, relative[k] * BASE + rank, -1),
                jnp.where(rank < BASE, -1, relative[k] * rest + rank - BASE),
            )
        )
    return keys


def exchange_kernel(
    experts, rest, fold, s_fold, chunks,
    routes_hbm, weights_hbm, rows_hbm, saved_hbm, w_hbm,
    pre_out, gate_out, down,
    routes, weights, rows, saved, w, pack, raw, names_in, relay_pick, relay, x_far, x, z,
    scaled, s_pack, s, s_wide, s_rest, s_turn, s_far, px_out, px_in, c_wide, c, r, c_routes, picks,
    grad_gate_factor, grad_up_factor, plain, key_col, left_col, weight_col, gate_col, total,
    load_sem, tn, rn, tw, rw, tm, rm, tg, rg, tss, rss, tf, rf, tp, rp, tb, rb,
):
    d = lax.axis_index("dp")
    e = lax.axis_index("expert")
    other = 1 - d
    me = d * experts + e
    half_experts = experts // 2
    at = e % half_experts
    near = (e // half_experts) * half_experts
    far = half_experts - near
    quarter = half_experts // 2
    lane, plane = at % quarter, at // quarter
    capacity = BASE + rest
    wide = 2 * capacity
    slab = relay_pick.shape[1] // half_experts
    gateway = quarter * (1 + far // half_experts) + lane
    is_gateway = (e // quarter) % 3 != 0
    tokens, width = rows.shape
    half = width // 2
    part = half // fold
    hidden = w.shape[0]
    part_s = hidden // s_fold
    group = half_experts * BASE
    rest_group = half_experts * rest
    count = experts * BASE

    def block(i):
        return pl.ds(pl.multiple_of(i * BASE, BASE), BASE)

    def remote(src, dst, send, recv, to):
        return pltpu.make_async_remote_copy(
            src_ref=src, dst_ref=dst, send_sem=send, recv_sem=recv, device_id=to, device_id_type=MESH
        )

    def wait_bytes(ref, sem):
        pltpu.make_async_copy(ref, ref, sem).wait()

    def loop(first, last, body):
        def step(k, carry):
            body(k)
            return carry

        lax.fori_loop(first, last, step, 0)

    loads = [
        pltpu.make_async_copy(source, target, load_sem.at[i])
        for i, (source, target) in enumerate(
            (
                (routes_hbm, routes), (rows_hbm, rows), (weights_hbm, weights), (saved_hbm, saved),
                (w_hbm, w),
            )
        )
    ]
    for load in loads:
        load.start()
    barrier = pltpu.get_barrier_semaphore()

    def greet(k):
        p = (me + k) % (2 * experts)
        pl.semaphore_signal(
            barrier, inc=1, device_id=(p // experts, p % experts), device_id_type=MESH
        )

    loop(1, 2 * experts, greet)

    loads[0].wait()
    (key0, left0), (key1, left1) = slot_keys(experts, rest, far, routes[...])
    row = iota((group, tokens), 0)
    main_pick = ((key0 == row + group) | (key1 == row + group)).astype(BF16)
    slot = (row // BASE) * rest + row % rest + rest_group
    hit = (left0 == slot) | (left1 == slot)
    left_pick = jnp.concatenate(
        [(hit & ((row // rest) % fold == q)).astype(BF16) for q in range(fold)], axis=1
    )

    def columns_of(h, lo, size):
        return pl.ds(pl.multiple_of(h * half + lo, 128), size)

    def pack_half(side, h):
        for lo in range(0, half, 512):
            pack[side, :, lo : lo + 512] = dot(
                main_pick, rows[:, columns_of(h, lo, 512)], ((1,), (0,))
            ).astype(BF16)
        folded = jnp.concatenate([rows[:, columns_of(h, q * part, part)] for q in range(fold)], axis=0)
        pack[side, :, half : half + part] = dot(left_pick, folded, ((1,), (0,))).astype(BF16)

    def near_copy(side, j):
        return remote(
            pack.at[side, block(j)],
            x.at[block(side * half_experts + at)],
            tn.at[side],
            rn.at[side],
            (other if side == 0 else d, near + j),
        )

    chunk, ahead, lead = half // chunks, 8, 6
    order = [(0, n) for n in range(lead)]
    for n in range(chunks):
        order += [(0, n + lead)] * (n + lead < chunks) + [(1, n)]

    def raw_copy(side, n):
        h = other if side == 0 else d
        return remote(
            rows.at[:, columns_of(h, n * chunk, chunk)],
            raw.at[side, pl.ds(pl.multiple_of(plane * tokens, tokens), tokens), n * chunk : (n + 1) * chunk],
            tw.at[side * chunks + n],
            rw.at[side * chunks + n],
            (h, gateway),
        )

    def names_copy(side):
        h = other if side == 0 else d
        return remote(routes, names_in.at[2 * side + plane], tm.at[0], rm.at[0], (h, gateway))

    loads[1].wait()
    pack_half(0, other)
    pack_half(1, d)
    pl.semaphore_wait(barrier, 2 * experts - 1)
    for side in range(2):
        names_copy(side).start()
    for side, n in order[:ahead]:
        raw_copy(side, n).start()

    def each_near(body):
        for k in range(quarter):
            for p in range(2):
                j = (plane if p == 0 else 1 - plane) * quarter + (lane + k) % quarter
                body(j, k == 0 and p == 0)

    def start_near_own(j, is_self):
        if not is_self:
            near_copy(1, j).start()

    def start_near_across(j, is_self):
        near_copy(0, j).start()

    each_near(start_near_own)
    pltpu.make_async_copy(
        pack.at[1, block(at)], x.at[block(half_experts + at)], rn.at[1]
    ).start()

    token_of = iota((2 * tokens, tokens), 0) // 2 == iota((2 * tokens, tokens), 1)
    first = iota((2 * tokens, tokens), 0) % 2 == 0

    def column(v0, v1):
        value = jnp.where(first, v0.astype(F32), v1.astype(F32))
        return jnp.sum(jnp.where(token_of, value, 0.0), axis=1, keepdims=True)

    loads[2].wait()
    key_col[...] = column(key0, key1).astype(jnp.int32)
    left_col[...] = column(left0, left1).astype(jnp.int32)
    weight_col[...] = column(weights[0:1, :], weights[1:2, :])
    loads[3].wait()
    step = 16

    @pl.loop(0, tokens // step)
    def _(i):
        mine = pl.ds(pl.multiple_of(i * 2 * step, 2 * step), 2 * step)
        both = saved[pl.ds(pl.multiple_of(i * step, step), step)].reshape(2 * step, 2 * hidden)
        gate_pre = both[:, :hidden].astype(F32)
        up_pre = both[:, hidden:].astype(F32)
        sigma = jax.nn.sigmoid(gate_pre)
        active = gate_pre * sigma
        weight = weight_col[mine, :]
        plain[mine, :] = (active * up_pre).astype(BF16)
        scaled[mine, :] = (weight * active * up_pre).astype(BF16)
        grad_up_factor[mine, :] = weight * active
        grad_gate_factor[mine, :] = weight * up_pre * sigma * (1.0 + gate_pre * (1.0 - sigma))

    slots = iota((2 * tokens, count), 1)

    picks[0] = (key_col[...] == slots).astype(BF16)
    wanted = (slots // BASE) * rest + slots % rest
    hit = left_col[...] == wanted
    for q in range(s_fold):
        picks[1 + q] = (hit & ((slots // rest) % fold == q)).astype(BF16)

    s_pack[:, 0:hidden] = dot(picks[0], scaled[...], ((0,), (0,))).astype(BF16)
    folded = jnp.zeros((count, part_s), F32)
    for q in range(s_fold):
        folded = folded + dot(
            picks[1 + q], scaled[:, q * part_s : (q + 1) * part_s], ((0,), (0,))
        )
    s_pack[:, hidden : hidden + part_s] = folded.astype(BF16)

    def scaled_copy(is_far, j):
        g = 1 if is_far else 3
        n = 1 + at if is_far else 0
        source = s_pack.at[block(j if is_far else half_experts + j)]
        to = (d, (far if is_far else near) + j)
        return remote(source, s.at[block(g * half_experts + at)], tss.at[int(is_far)], rss.at[n], to)

    def back_copy(is_far, j):
        n = 0 if is_far else 1
        source = c.at[block(j if is_far else half_experts + j)]
        to = (d, (far if is_far else near) + j)
        return remote(source, r.at[block(n * half_experts + at)], tb.at[n], rb.at[n], to)

    def rows_of(g):
        return slice(g * group, (g + 1) * group)

    def rest_of(g):
        return slice(g * rest_group, (g + 1) * rest_group)

    def slots_of(side):
        return slice(side * quarter * wide, (side + 1) * quarter * wide)

    def wide_pick(q, turned):
        shape = (quarter * wide, group) if turned else (group, quarter * wide)
        narrow, there = iota(shape, int(turned)), iota(shape, 1 - int(turned))
        source, inner = narrow // BASE, narrow % BASE
        base = (source % quarter) * wide + (source // quarter) * capacity
        if q is None:
            return (there == base + inner).astype(BF16)
        return ((there == base + BASE + inner % rest) & (inner // rest == q)).astype(BF16)

    def contract(n, side, put):
        if n == 0:
            lanes = slice(side * quarter, (side + 1) * quarter)
            wait_bytes(x_far.at[lanes], rg.at[side])
            lhs = x_far[lanes].reshape(quarter * wide, half)
        else:
            wait_bytes(x.at[rows_of(side)], rn.at[side])
            for q in range(fold):
                z[rest_of(side), q * part : (q + 1) * part] = dot(
                    unfold_pick(half_experts, rest, q),
                    x[rows_of(side), half : half + part],
                    ((1,), (0,)),
                ).astype(BF16)
            lhs = jnp.concatenate([x[rows_of(side), 0:half], z[rest_of(side), :]], axis=0)
        for lo in range(0, hidden, 256):
            put(lo, dot(lhs, w[lo : lo + 256, :], ((1,), (1,))))

    across = (other, e)

    def partial_copy(n):
        return remote(px_out.at[n], px_in.at[n], tp.at[n], rp.at[n], across)

    def forward_near():
        return remote(s.at[rows_of(3)], s.at[rows_of(2)], tf.at[0], rf.at[0], across)

    def forward_far(j):
        return remote(
            s.at[block(half_experts + j)], s.at[block(j)], tf.at[1 + j], rf.at[1 + j], across
        )

    loads[4].wait()

    def send_partial(n):
        def put(lo, value):
            px_out[n, :, lo : lo + 256] = value.astype(BF16)

        contract(n, 0, put)
        partial_copy(n).start()

    def finish(n):
        def put(lo, value):
            cut = slice(lo, lo + 256)
            summed = (value + px_in[n, :, cut].astype(F32)).astype(BF16)
            if n == 0:
                c_wide[:, cut] = summed
            else:
                c[rows_of(n), cut] = summed[:group]
                c_wide[0:rest_group, cut] = summed[group:]

        partial_copy(n).wait_recv()
        contract(n, 1, put)
        if n == 0:
            c[rows_of(n), 0:hidden] = dot(
                wide_pick(None, False), c_wide[...], ((1,), (0,))
            ).astype(BF16)
        folded = jnp.zeros((group, part_s), F32)
        for q in range(s_fold):
            cut = slice(q * part_s, (q + 1) * part_s)
            if n == 0:
                folded = folded + dot(wide_pick(q, False), c_wide[:, cut], ((1,), (0,)))
            else:
                folded = folded + dot(
                    fold_pick(half_experts, rest, fold, q), c_wide[0:rest_group, cut], ((1,), (0,))
                )
        c[rows_of(n), hidden : hidden + part_s] = folded.astype(BF16)

    def relay_copy(side, n, j):
        return remote(
            relay.at[side, n, j],
            x_far.at[side * quarter + lane, :, n * chunk : (n + 1) * chunk],
            tg.at[0],
            rg.at[side],
            (d, near + j),
        )

    def build_relay_pick():
        wait_bytes(names_in, rm.at[0])
        before = (iota((tokens, tokens), 0) < iota((tokens, tokens), 1)).astype(BF16)
        names = iota((half_experts, tokens), 0)
        target = iota((half_experts * slab, tokens), 0)
        for side in range(2):
            for p in range(2):
                named = [names_in[2 * side + p, k : k + 1, :] - near for k in range(2)]
                onehot = [(named[k] == names).astype(F32) for k in range(2)]
                counts = dot((onehot[0] + onehot[1]).astype(BF16), before, ((1,), (0,)))
                hits = []
                for k in range(2):
                    rank = jnp.sum(counts * onehot[k], axis=0, keepdims=True).astype(jnp.int32)
                    here = (named[k] >= 0) & (named[k] < half_experts)
                    hits.append(target == jnp.where(here, named[k] * slab + p * capacity + rank, -1))
                relay_pick[side, :, p * tokens : (p + 1) * tokens] = (hits[0] | hits[1]).astype(BF16)

    def relay_step(side, n):
        cut = slice(n * chunk, (n + 1) * chunk)
        wait_bytes(raw.at[side, :, cut], rw.at[side * chunks + n])
        packed = dot(relay_pick[side], raw[side, :, cut], ((1,), (0,))).astype(BF16)
        for j in range(half_experts):
            relay[side, n, j] = packed[j * slab : j * slab + wide]

        def start(j, is_self):
            if not is_self:
                relay_copy(side, n, j).start()

        each_near(start)
        pltpu.make_async_copy(
            relay.at[side, n, at],
            x_far.at[side * quarter + lane, :, cut],
            rg.at[side],
        ).start()

    def raw_steps(first, last):
        for i in range(first, last):

            @pl.when(is_gateway)
            def _():
                relay_step(*order[i])

            raw_copy(*order[i]).wait_send()
            if i + ahead < len(order):
                raw_copy(*order[i + ahead]).start()

    def scaled_start(is_far):
        def start(k):
            scaled_copy(is_far, (at + k) % half_experts).start()

        loop(0 if is_far else 1, half_experts, start)

    pl.when(is_gateway)(build_relay_pick)
    scaled_start(False)
    pltpu.make_async_copy(
        s_pack.at[block(half_experts + at)], s.at[block(3 * half_experts + at)], rss.at[0]
    ).start()
    raw_steps(0, 7)
    each_near(start_near_across)
    wait_bytes(s.at[rows_of(3)], rss.at[0])
    forward_near().start()
    raw_steps(7, 14)
    send_partial(0)
    raw_steps(14, 16)
    send_partial(1)
    scaled_start(True)
    finish(0)
    def start_back_far(k):
        back_copy(True, (at + k) % half_experts).start()

    loop(0, half_experts, start_back_far)

    finish(1)
    def start_back_near(k):
        back_copy(False, (at + k) % half_experts).start()

    loop(1, half_experts, start_back_near)
    pltpu.make_async_copy(
        c.at[block(half_experts + at)], r.at[block(half_experts + at)], rb.at[1]
    ).start()


    def widen(side):
        for q in range(s_fold):
            cut = slice(q * part_s, (q + 1) * part_s)
            s_wide[slots_of(side), cut] = (
                dot(wide_pick(None, True), s[rows_of(side), cut], ((1,), (0,)))
                + dot(wide_pick(q, True), s[rows_of(side), hidden : hidden + part_s], ((1,), (0,)))
            ).astype(BF16)

    def turn_near():
        for side in range(2):
            for q in range(s_fold):
                s_rest[rest_of(side), q * part_s : (q + 1) * part_s] = dot(
                    unfold_pick(half_experts, rest, q),
                    s[rows_of(2 + side), hidden : hidden + part_s],
                    ((1,), (0,)),
                ).astype(BF16)
        s_turn[:, 0 : 2 * group] = s[2 * group : 4 * group, 0:hidden].T
        s_turn[:, 2 * group : 2 * group + 2 * rest_group] = s_rest[...].T

    def near_product(columns):
        return dot(s_turn[:, 0 : 2 * group], x[:, columns], ((1,), (0,))) + dot(
            s_turn[:, 2 * group : 2 * group + 2 * rest_group], z[:, columns], ((1,), (0,))
        )

    def far_product(side, columns):
        rhs = x_far[side * quarter : (side + 1) * quarter, :, columns]
        return dot(s_far[side], rhs.reshape(quarter * wide, columns.size), ((1,), (0,)))

    def each_columns(body):
        @pl.loop(0, half // 512)
        def _(j):
            body(pl.ds(pl.multiple_of(j * 512, 512), 512))

    forward_near().wait_recv()
    turn_near()

    def add_near(columns):
        total[:, columns] = near_product(columns)

    each_columns(add_near)

    def pass_on(k):
        j = (at + half_experts - k) % half_experts
        wait_bytes(s.at[block(half_experts + j)], rss.at[1 + j])
        forward_far(j).start()

    loop(0, half_experts, pass_on)
    widen(1)
    s_far[1] = s_wide[slots_of(1), :].T

    def add_own(columns):
        total[:, columns] = total[:, columns] + far_product(1, columns)

    each_columns(add_own)
    loop(0, half_experts, lambda j: forward_far(j).wait_recv())
    widen(0)
    s_far[0] = s_wide[slots_of(0), :].T

    def add_across(columns):
        down[:, columns] = (total[:, columns] + far_product(0, columns)).astype(BF16)

    each_columns(add_across)

    def unpermuted(n, q):
        cut = slice(q * part_s, (q + 1) * part_s)
        return dot(picks[0, :, rows_of(n)], r[rows_of(n), cut], ((1,), (0,))) + dot(
            picks[1 + q, :, rows_of(n)], r[rows_of(n), hidden : hidden + part_s], ((1,), (0,))
        )

    wait_bytes(r.at[rows_of(1)], rb.at[1])
    for q in range(s_fold):
        c_routes[:, q * part_s : (q + 1) * part_s] = unpermuted(1, q)
    wait_bytes(r.at[rows_of(0)], rb.at[0])
    for q in range(s_fold):
        cut = slice(q * part_s, (q + 1) * part_s)
        c_routes[:, cut] = c_routes[:, cut] + unpermuted(0, q)

    @pl.loop(0, tokens // step)
    def _(i):
        mine = pl.ds(pl.multiple_of(i * 2 * step, 2 * step), 2 * step)
        value = c_routes[mine, :]
        gate_col[mine, :] = jnp.sum(plain[mine, :].astype(F32) * value, axis=1, keepdims=True)
        out = jnp.concatenate(
            [value * grad_gate_factor[mine, :], value * grad_up_factor[mine, :]], axis=1
        ).astype(BF16)
        pre_out[pl.ds(pl.multiple_of(i * step, step), step)] = out.reshape(step, 2, 2 * hidden)

    for k in range(2):
        mine = token_of & (first if k == 0 else ~first)
        gate_out[k : k + 1, :] = jnp.sum(
            jnp.where(mine, gate_col[...], 0.0), axis=0, keepdims=True
        ).astype(BF16)

    wait_bytes(pack.at[0], tn.at[0])
    wait_bytes(pack.at[1, 0 : group - BASE], tn.at[1])
    wait_bytes(names_in.at[0:2], tm.at[0])

    @pl.when(is_gateway)
    def _():
        wait_bytes(relay.at[:, :, 0 : half_experts - 1], tg.at[0])

    wait_bytes(s_pack.at[0:group], tss.at[1])
    wait_bytes(s_pack.at[group : 2 * group - BASE], tss.at[0])
    wait_bytes(c.at[0:group], tb.at[0])
    wait_bytes(c.at[group : 2 * group - BASE], tb.at[1])
    for n in range(2):
        partial_copy(n).wait_send()
    forward_near().wait_send()
    loop(0, half_experts, lambda j: forward_far(j).wait_send())


def store_kernel(*refs):
    copies = [pltpu.make_async_copy(refs[i], refs[3 + i], refs[6].at[i]) for i in range(3)]
    for copy in copies:
        copy.start()
    for copy in copies:
        copy.wait()


def on_device(grad_out, saved_pre, gate_weight, routes, w_down):
    tokens, top_count = routes.shape
    hidden, half = w_down.shape[1:]
    width = grad_out.shape[1]
    experts = lax.axis_size("expert")
    replicas = lax.axis_size("dp")
    capacity = 5 * tokens * top_count // (4 * experts)
    if (replicas, top_count, experts, capacity, hidden, half % 512) != (2, 2, 16, 20, 768, 0):
        return on_device_general(grad_out, saved_pre, gate_weight, routes, w_down)
    rest = capacity - BASE
    fold = BASE // rest
    s_fold = hidden // 256
    devices = replicas * experts
    count, total = experts * BASE, devices * BASE
    part, part_s = half // fold, hidden // s_fold
    finished = (count + experts * rest) // 2
    chunks = half // 256
    vmem = pl.BlockSpec(memory_space=pltpu.VMEM)
    stored = pl.BlockSpec(memory_space=pltpu.HBM)
    dma = pltpu.SemaphoreType.DMA
    pre, gate, down = pl.pallas_call(
        functools.partial(exchange_kernel, experts, rest, fold, s_fold, chunks),
        out_shape=(
            pltpu.VMEM(saved_pre.shape, BF16),
            pltpu.VMEM((top_count, tokens), BF16),
            pltpu.VMEM((hidden, half), BF16),
        ),
        in_specs=[stored] * 5,
        out_specs=[vmem] * 3,
        scratch_shapes=[
            pltpu.VMEM((top_count, tokens), jnp.int32),
            pltpu.VMEM((top_count, tokens), BF16),
            pltpu.VMEM((tokens, width), BF16),
            pltpu.VMEM(saved_pre.shape, BF16),
            pltpu.VMEM((hidden, half), BF16),
            pltpu.VMEM((2, count // 2, half + part), BF16),
            pltpu.VMEM((2, 2 * tokens, half), BF16),
            pltpu.VMEM((4, top_count, tokens), jnp.int32),
            pltpu.VMEM((2, experts // 2 * -(-2 * capacity // 16) * 16, 2 * tokens), BF16),
            pltpu.VMEM((2, chunks, experts // 2, 2 * capacity, half // chunks), BF16),
            pltpu.VMEM((experts // 2, 2 * capacity, half), BF16),
            pltpu.VMEM((count, half + part), BF16),
            pltpu.VMEM((experts * rest, half), BF16),
            pltpu.VMEM((2 * tokens, hidden), BF16),
            pltpu.VMEM((count, hidden + part_s), BF16),
            pltpu.VMEM((total, hidden + part_s), BF16),
            pltpu.VMEM((2 * finished, hidden), BF16),
            pltpu.VMEM((experts * rest, hidden), BF16),
            pltpu.VMEM((hidden, 2 * finished), BF16),
            pltpu.VMEM((2, hidden, finished), BF16),
            pltpu.VMEM((2, finished, hidden), BF16),
            pltpu.VMEM((2, finished, hidden), BF16),
            pltpu.VMEM((finished, hidden), BF16),
            pltpu.VMEM((count, hidden + part_s), BF16),
            pltpu.VMEM((count, hidden + part_s), BF16),
            pltpu.VMEM((2 * tokens, hidden), F32),
            pltpu.VMEM((1 + s_fold, 2 * tokens, count), BF16),
            pltpu.VMEM((2 * tokens, hidden), F32),
            pltpu.VMEM((2 * tokens, hidden), F32),
            pltpu.VMEM((2 * tokens, hidden), BF16),
            pltpu.VMEM((2 * tokens, 1), jnp.int32),
            pltpu.VMEM((2 * tokens, 1), jnp.int32),
            pltpu.VMEM((2 * tokens, 1), F32),
            pltpu.VMEM((2 * tokens, 1), F32),
            pltpu.VMEM((hidden, half), F32),
            dma((5,)),
            dma((2,)), dma((2,)), dma((2 * chunks,)), dma((2 * chunks,)), dma((1,)), dma((1,)),
            dma((1,)), dma((2,)),
            dma((2,)), dma((experts,)), dma((experts,)), dma((experts,)),
            dma((2,)), dma((2,)), dma((2,)), dma((2,)),
        ],
        compiler_params=pltpu.CompilerParams(
            collective_id=0, has_side_effects=True, vmem_limit_bytes=40 << 20
        ),
    )(*[
        pltpu.with_memory_space_constraint(operand, pltpu.HBM)
        for operand in (routes.T, gate_weight.T, grad_out, saved_pre, w_down[0])
    ])
    pre, gate, down = pl.pallas_call(
        store_kernel,
        out_shape=[jax.ShapeDtypeStruct(a.shape, a.dtype) for a in (pre, gate, down)],
        in_specs=[vmem] * 3,
        out_specs=[stored] * 3,
        scratch_shapes=[dma((3,))],
        compiler_params=pltpu.CompilerParams(vmem_limit_bytes=1 << 20),
    )(pre, gate, down)
    return pre, gate.T, down[None]


def solution(mesh):
    return jax.shard_map(
        on_device,
        mesh=mesh,
        in_specs=(
            P(("dp", "expert"), None),
            P(("dp", "expert"), None, None),
            P(("dp", "expert"), None),
            P(("dp", "expert"), None),
            P("expert", None, "dp"),
        ),
        out_specs=(
            P(("dp", "expert"), None, None),
            P(("dp", "expert"), None),
            P("expert", None, "dp"),
        ),
        check_vma=False,
    )
```
